256 devices in a mesh: seq: 8 (over x, core), dp: 8 (over z), fsdp: 4 (over y).
Axes of the slice: x: 4, y: 4, z: 8, core: 2. Of those that a mesh axis runs over, the one named last changes fastest.
Arguments:
- query_rows: bfloat16 [32, 1024, 4096], P(('dp', 'fsdp'), 'seq'), may hold values from -2.5 to 2.5
- forward_key_rows: bfloat16 [32, 1024, 1024], P(('dp', 'fsdp'), 'seq'), may hold values from -2.5 to 2.5
- forward_value_rows: bfloat16 [32, 1024, 1024], P(('dp', 'fsdp'), 'seq'), may hold values from -4 to 4
- out_cotangent: bfloat16 [32, 1024, 4096], P(('dp', 'fsdp'), 'seq'), may hold values from -12 to 12
- proj_weight: bfloat16 [4096, 4096], P(('dp', 'fsdp'), 'seq'), may hold values from -0.09375 to 0.09375
- sent_lengths: int32 [32, 32], P(('dp', 'fsdp')), may hold values from 1 to 64, 1024 in all within a row
Outputs:
- query_grad: bfloat16 [32, 1024, 4096], P(('dp', 'fsdp'), 'seq')
- key_gradient: bfloat16 [32, 1024, 1024], P(('dp', 'fsdp'), 'seq')
- value_gradient: bfloat16 [32, 1024, 1024], P(('dp', 'fsdp'), 'seq')
- proj_grad: bfloat16 [4096, 4096], P(('dp', 'fsdp'), 'seq')
The draws below stay inside these ranges and needn't reach their ends.
Inputs may be any that keep to these rules, and one draw needn't show every extreme that they name: `sent_lengths`: each window's 32 lengths sum to 1024, and the longest is exactly 64.
All inputs are finite; a program needn't handle non-finite values.
Results may differ from the reference program's by a relative error of at most 0.0058.
Values may be sent and summed in bfloat16 or wider, within the bound.
No kernel may reach another device: no remote copies, remote signals or barrier semaphores. Data moves between devices by JAX's collectives and lax.ppermute only.
A program may use at most 128 MiB of HBM per device.

```python
import math
import jax
import jax.numpy as jnp
import numpy as np
from jax import lax

D = 4096
QUERY_HEADS = 32
KEY_VALUE_HEADS = 8
HEAD_SIZE = 128
WINDOW_LENGTH = 1024
SENTS = 32
MOST = 64
WINDOW_COUNT = 32


def spiked(array, own_key, source, target, blocks, factor):
    owner, partner = [(jnp.arange(array.shape[dim]) // (array.shape[dim] // blocks)).reshape([-1 if axis == dim else 1 for axis in range(array.ndim)]) for dim in (source, target)]
    chosen = jax.random.permutation(own_key, blocks)[partner]
    strong = (owner == chosen) | (owner == (partner + blocks // 2) % blocks)
    return jnp.where(strong, factor * array, array)


def shard_levels(rng, extent, split, smallest, top_value):
    def one(axis_at, parts):
        draws = jax.random.uniform(jax.random.fold_in(jax.random.fold_in(rng, 6), axis_at), (parts,), jnp.float32, smallest / len(split), top_value / len(split))
        return jnp.repeat(jnp.exp(draws), extent[axis_at] // parts).reshape((-1,) + (1,) * (len(extent) - axis_at - 1))

    level = one(*split[0])
    for cut in split[1:]:
        level = level * one(*cut)
    return level


def split_up(amount, total, limit, lean):
    weights = [(1 << 20) // math.isqrt(grade ** lean) + 1 for grade in range(2, amount + 1)]
    surplus, holding = total - limit - (amount - 1), [1] * (amount - 1)
    while surplus > 0:
        free = [i for i in range(amount - 1) if holding[i] < limit]
        pool, budget = sum([weights[i] for i in free]), surplus
        for i in free:
            extra = min(limit - holding[i], max(1, budget * weights[i] // pool), surplus)
            holding[i] = holding[i] + extra
            surplus = surplus - extra
    return np.array([limit] + holding)


def uneven_parts(own_key, number_of, total, reach, lean):
    if number_of == 2:
        one = jax.random.randint(own_key, (), max(1, total - reach), min(reach, total - 1) + 1)
        return jnp.stack([one, total - one])
    sizes = jnp.asarray(split_up(number_of, total, reach, lean), jnp.int32)
    couples = (number_of - 1) // 2
    giver, receiver = sizes[1:1 + 2 * couples:2], sizes[2:2 + 2 * couples:2]
    room = jnp.minimum(giver - 1, reach - receiver)
    moved = jax.random.randint(jax.random.fold_in(own_key, 1), (couples,), 0, 1 << 20) % (room + 1)
    sizes = sizes.at[1:1 + 2 * couples:2].set(giver - moved).at[2:2 + 2 * couples:2].set(receiver + moved)
    return sizes[jax.random.permutation(jax.random.fold_in(own_key, 2), number_of)]


def centred(rng, shape, spread, limit, shards=(), held_as=jnp.bfloat16):
    drawn = spread * jax.random.normal(rng, shape, jnp.float32)
    if shards:
        drawn = drawn * shard_levels(rng, shape, shards, -0.22, 0.18)
    return jnp.clip(drawn, -limit, limit).astype(held_as)


def heavy_noise(key, extent, deviation, most, shards, heavy, kind=jnp.bfloat16):
    values = deviation * jax.random.normal(key, extent, jnp.float32)
    if shards:
        values = values * shard_levels(key, extent, shards, -0.22, 0.18)
    return jnp.clip(spiked(values, jax.random.fold_in(key, 3), *heavy), -most, most).astype(kind)


def setup_inputs(seed: int = 0) -> dict:
    key_list = jax.random.split(jax.random.key(seed), 7)
    query_rows = centred(key_list[0], (WINDOW_COUNT, WINDOW_LENGTH, QUERY_HEADS * HEAD_SIZE), 1.0, 2.5, ((0, 32), (1, 8)))
    forward_key_rows = centred(key_list[1], (WINDOW_COUNT, WINDOW_LENGTH, KEY_VALUE_HEADS * HEAD_SIZE), 1.0, 2.5, ((0, 32), (1, 8)))
    forward_value_rows = centred(key_list[2], (WINDOW_COUNT, WINDOW_LENGTH, KEY_VALUE_HEADS * HEAD_SIZE), 1.0, 4.0, ((0, 32), (1, 8)))
    out_cotangent = heavy_noise(key_list[3], (WINDOW_COUNT, WINDOW_LENGTH, D), 1.0, 12.0, ((0, 32), (1, 8)), (0, 2, 32, 2.75))
    proj_weight = centred(key_list[4], (D, QUERY_HEADS * HEAD_SIZE), (QUERY_HEADS * HEAD_SIZE) ** -0.5, 0.09375, ((0, 32), (1, 8)))
    sent_lengths = jax.vmap(lambda own: uneven_parts(own, SENTS, WINDOW_LENGTH, MOST, 1))(jax.random.split(key_list[5], WINDOW_COUNT)).reshape((WINDOW_COUNT, SENTS)).astype(jnp.int32)
    return dict(query_rows=query_rows, forward_key_rows=forward_key_rows, forward_value_rows=forward_value_rows, out_cotangent=out_cotangent, proj_weight=proj_weight, sent_lengths=sent_lengths)


def sentence_ids(length_row):
    bounds = jnp.cumsum(length_row).astype(jnp.int32)
    places = jnp.arange(WINDOW_LENGTH, dtype=jnp.int32)
    return lax.optimization_barrier(jnp.sum((places[:, None] >= bounds[None, :]).astype(jnp.int32), axis=1)).astype(jnp.int32)

def reference(query_rows, forward_key_rows, forward_value_rows, out_cotangent, proj_weight, sent_lengths):
    queries_per_group = QUERY_HEADS // KEY_VALUE_HEADS
    factor = 1.0 / math.sqrt(HEAD_SIZE)

    def window(running, inputs):
        query_matrix, every_key_row, every_value_row, cotangent, length_row = inputs
        sentence = sentence_ids(length_row)
        allowed = (sentence[None, :] <= sentence[:, None]) & (sentence[None, :] >= sentence[:, None] - 3)
        upstream_gradient = jnp.dot(cotangent, proj_weight, preferred_element_type=jnp.float32).astype(jnp.bfloat16)
        upstream_gradient = lax.optimization_barrier(upstream_gradient)
        heads_of_queries = query_matrix.reshape(WINDOW_LENGTH, KEY_VALUE_HEADS, queries_per_group, HEAD_SIZE).transpose(1, 2, 0, 3)
        heads_of_keys = every_key_row.reshape(WINDOW_LENGTH, KEY_VALUE_HEADS, HEAD_SIZE).transpose(1, 0, 2)
        heads_of_values = every_value_row.reshape(WINDOW_LENGTH, KEY_VALUE_HEADS, HEAD_SIZE).transpose(1, 0, 2)
        heads_of_upstream = upstream_gradient.reshape(WINDOW_LENGTH, KEY_VALUE_HEADS, queries_per_group, HEAD_SIZE).transpose(1, 2, 0, 3)

        def one_head(pieces):
            query_wide = pieces[0].astype(jnp.float32)
            key_wide = pieces[1].astype(jnp.float32)
            value_wide = pieces[2].astype(jnp.float32)
            upstream_wide = pieces[3].astype(jnp.float32)
            scores = jnp.einsum('hqd,kd->hqk', query_wide, key_wide) * factor
            raised = jnp.where(allowed[None], jnp.exp(scores), 0.0)
            attend = raised / lax.optimization_barrier(jnp.sum(raised, axis=-1, keepdims=True))
            rounded = lax.optimization_barrier(attend.astype(jnp.bfloat16)).astype(jnp.float32)
            output = jnp.einsum('hqk,kd->hqd', rounded, value_wide).astype(jnp.bfloat16)
            grad_attend = jnp.einsum('hqd,kd->hqk', upstream_wide, value_wide)
            dscore = attend * (grad_attend - lax.optimization_barrier(jnp.sum(attend * grad_attend, axis=-1, keepdims=True))) * factor
            dscore = lax.optimization_barrier(dscore.astype(jnp.bfloat16)).astype(jnp.float32)
            query_grad = jnp.einsum('hqk,kd->hqd', dscore, key_wide).astype(jnp.bfloat16)
            key_gradient = jnp.einsum('hqk,hqd->kd', dscore, query_wide).astype(jnp.bfloat16)
            value_gradient = jnp.einsum('hqk,hqd->kd', rounded, upstream_wide).astype(jnp.bfloat16)
            return (output, query_grad, key_gradient, value_gradient)
        result_list = lax.map(one_head, (heads_of_queries, heads_of_keys, heads_of_values, heads_of_upstream))
        output = result_list[0].transpose(2, 0, 1, 3).reshape(WINDOW_LENGTH, QUERY_HEADS * HEAD_SIZE)
        query_grad = result_list[1].transpose(2, 0, 1, 3).reshape(WINDOW_LENGTH, QUERY_HEADS * HEAD_SIZE)
        key_gradient = result_list[2].transpose(1, 0, 2).reshape(WINDOW_LENGTH, KEY_VALUE_HEADS * HEAD_SIZE)
        value_gradient = result_list[3].transpose(1, 0, 2).reshape(WINDOW_LENGTH, KEY_VALUE_HEADS * HEAD_SIZE)
        running = running + jnp.dot(cotangent.T, output, preferred_element_type=jnp.float32)
        return (running, (query_grad, key_gradient, value_gradient))
    starting = jnp.zeros((D, QUERY_HEADS * HEAD_SIZE), jnp.float32)
    summed, gradients = lax.scan(window, starting, (query_rows, forward_key_rows, forward_value_rows, out_cotangent, sent_lengths))
    return (gradients[0], gradients[1], gradients[2], summed.astype(jnp.bfloat16))
```

```python
import math

import jax
import jax.numpy as jnp
from jax import lax
from jax.experimental import pallas as pl
from jax.experimental.pallas import tpu as pltpu
from jax.sharding import PartitionSpec as P

HEADS = 4
HEAD = 128
TOK = 128
KW = 448
FACTOR = 1.0 / math.sqrt(HEAD)
F32 = jnp.float32
BF16 = jnp.bfloat16
GROUP = 2
GRID = {"dp": 8, "fsdp": 4}


def window_start(i, blocks):
    return pl.multiple_of(jnp.clip(i * TOK - 256, 0, blocks * TOK - KW), 64)


def probs(i, start, g_ref, lo_ref, hi_ref, key, h0):
    q = jnp.concatenate(
        [g_ref[i, :, (h0 + j) * HEAD : (h0 + j + 1) * HEAD] for j in range(GROUP)], 0
    )
    s = lax.dot_general(key, q, (((1,), (1,)), ((), ())), preferred_element_type=F32)
    place = start + lax.broadcasted_iota(jnp.int32, (KW, GROUP * TOK), 0)
    lo = jnp.concatenate([lo_ref[i]] * GROUP, 1)
    hi = jnp.concatenate([hi_ref[i]] * GROUP, 1)
    p = jnp.where((place >= lo) & (place < hi), jnp.exp(s * FACTOR), 0.0)
    a = p * (1.0 / jnp.sum(p, axis=0, keepdims=True))
    return q, a


def unpack_keys(g_ref, k_ref, v_ref):
    for b in range(g_ref.shape[0]):
        rows = slice(b * TOK, (b + 1) * TOK)
        k_ref[rows, :] = g_ref[b, :, HEADS * HEAD : (HEADS + 1) * HEAD]
        v_ref[rows, :] = g_ref[b, :, (HEADS + 1) * HEAD :]


def fwd_kernel(g_ref, lo_ref, hi_ref, o_ref, k_ref, v_ref):
    blocks = g_ref.shape[0]
    i = pl.program_id(0)

    @pl.when(i == 0)
    def _():
        unpack_keys(g_ref, k_ref, v_ref)

    start = window_start(i, blocks)
    key = k_ref[pl.ds(start, KW), :]
    vt = v_ref[pl.ds(start, KW), :].T
    for h0 in range(0, HEADS, GROUP):
        _, a = probs(i, start, g_ref, lo_ref, hi_ref, key, h0)
        o = jnp.dot(vt, a.astype(BF16), preferred_element_type=F32).astype(BF16)
        for j in range(GROUP):
            o_ref[0, (h0 + j) * HEAD : (h0 + j + 1) * HEAD, :] = o[:, j * TOK : (j + 1) * TOK]


def bwd_kernel(g_ref, u_ref, lo_ref, hi_ref, o_ref, dk_ref, dv_ref, k_ref, v_ref):
    blocks = g_ref.shape[0]
    i = pl.program_id(0)

    @pl.when(i == 0)
    def _():
        unpack_keys(g_ref, k_ref, v_ref)
        dk_ref[...] = jnp.zeros_like(dk_ref)
        dv_ref[...] = jnp.zeros_like(dv_ref)

    start = window_start(i, blocks)
    key = k_ref[pl.ds(start, KW), :]
    val = v_ref[pl.ds(start, KW), :]
    kt = key.T
    dk = None
    for h0 in range(0, HEADS, GROUP):
        q, a = probs(i, start, g_ref, lo_ref, hi_ref, key, h0)
        u = jnp.concatenate(
            [u_ref[i, :, (h0 + j) * HEAD : (h0 + j + 1) * HEAD] for j in range(GROUP)], 0
        )
        g = lax.dot_general(val, u, (((1,), (1,)), ((), ())), preferred_element_type=F32)
        delta = jnp.sum(a * g, axis=0, keepdims=True)
        ds = (a * (g - delta) * FACTOR).astype(BF16)
        dq = jnp.dot(kt, ds, preferred_element_type=F32)
        for j in range(GROUP):
            o_ref[i, :, (h0 + j) * HEAD : (h0 + j + 1) * HEAD] = dq[
                :, j * TOK : (j + 1) * TOK
            ].T.astype(BF16)
        dkh = jnp.dot(ds, q, preferred_element_type=F32)
        dvh = jnp.dot(a.astype(BF16), u, preferred_element_type=F32)
        dk, dv = (dkh, dvh) if dk is None else (dk + dkh, dv + dvh)
    dk_ref[pl.ds(start, KW), :] += dk
    dv_ref[pl.ds(start, KW), :] += dv

    @pl.when(i == blocks - 1)
    def _():
        for b in range(blocks):
            o_ref[b, :, HEADS * HEAD : (HEADS + 1) * HEAD] = dk_ref[
                b * TOK : (b + 1) * TOK, :
            ].astype(BF16)
            o_ref[b, :, (HEADS + 1) * HEAD :] = dv_ref[b * TOK : (b + 1) * TOK, :].astype(BF16)


def whole(shape):
    return pl.BlockSpec(shape, lambda i: (0,) * len(shape))


def limits(sent_lengths, blocks):
    number = sent_lengths.shape[0]
    order = jnp.arange(number, dtype=jnp.int32)
    ends = jnp.sum(jnp.where(order[None, :] <= order[:, None], sent_lengths[None, :], 0), axis=1)
    places = jnp.arange(blocks * TOK, dtype=jnp.int32)
    sentence = jnp.sum((places[:, None] >= ends[None, :]).astype(jnp.int32), axis=1)
    lo = jnp.sum(
        jnp.where(order[None, :] + 3 < sentence[:, None], sent_lengths[None, :], 0), axis=1
    )
    hi = jnp.sum(jnp.where(order[None, :] <= sentence[:, None], sent_lengths[None, :], 0), axis=1)
    return lo.reshape(blocks, 1, TOK), hi.reshape(blocks, 1, TOK)


def attend(g, lo, hi):
    blocks = g.shape[0]
    pairs = blocks * TOK * KW * HEADS
    return pl.pallas_call(
        fwd_kernel,
        grid=(blocks,),
        in_specs=[whole(x.shape) for x in (g, lo, hi)],
        out_specs=pl.BlockSpec((1, HEADS * HEAD, TOK), lambda i: (i, 0, 0)),
        out_shape=jax.ShapeDtypeStruct((blocks, HEADS * HEAD, TOK), BF16),
        scratch_shapes=[pltpu.VMEM((blocks * TOK, HEAD), BF16)] * 2,
        cost_estimate=pl.CostEstimate(
            flops=4 * pairs * HEAD, bytes_accessed=4 * g.size, transcendentals=pairs
        ),
        name="attend",
    )(g, lo, hi)


def attend_grad(g, u, lo, hi):
    blocks = g.shape[0]
    pairs = blocks * TOK * KW * HEADS
    return pl.pallas_call(
        bwd_kernel,
        grid=(blocks,),
        in_specs=[whole(x.shape) for x in (g, u, lo, hi)],
        out_specs=whole(g.shape),
        out_shape=jax.ShapeDtypeStruct(g.shape, BF16),
        scratch_shapes=[pltpu.VMEM((blocks * TOK, HEAD), F32)] * 2
        + [pltpu.VMEM((blocks * TOK, HEAD), BF16)] * 2,
        cost_estimate=pl.CostEstimate(
            flops=10 * pairs * HEAD, bytes_accessed=6 * g.size, transcendentals=pairs
        ),
        name="attend_grad",
    )(g, u, lo, hi)


def pack_kernel(q_ref, k_ref, v_ref, o_ref):
    o_ref[0, :, : HEADS * HEAD] = q_ref[0]
    o_ref[0, :, HEADS * HEAD : (HEADS + 1) * HEAD] = k_ref[0]
    o_ref[0, :, (HEADS + 1) * HEAD :] = v_ref[0]


def head_specs():
    return [
        pl.BlockSpec((1, TOK, width), lambda i: (0, 0, i)) for width in (HEADS * HEAD, HEAD, HEAD)
    ]


def pack(q, k, v):
    groups = k.shape[2] // HEAD
    width = (HEADS + 2) * HEAD
    return pl.pallas_call(
        pack_kernel,
        grid=(groups,),
        in_specs=head_specs(),
        out_specs=pl.BlockSpec((1, TOK, width), lambda i: (i, 0, 0)),
        out_shape=jax.ShapeDtypeStruct((groups, TOK, width), BF16),
        cost_estimate=pl.CostEstimate(flops=0, bytes_accessed=8 * q.size, transcendentals=0),
        name="pack",
    )(q, k, v)


def unpack_kernel(i_ref, q_ref, k_ref, v_ref):
    q_ref[0] = i_ref[0, :, : HEADS * HEAD]
    k_ref[0] = i_ref[0, :, HEADS * HEAD : (HEADS + 1) * HEAD]
    v_ref[0] = i_ref[0, :, (HEADS + 1) * HEAD :]


def unpack(packed):
    groups, _, width = packed.shape
    return pl.pallas_call(
        unpack_kernel,
        grid=(groups,),
        in_specs=[pl.BlockSpec((1, TOK, width), lambda i: (i, 0, 0))],
        out_specs=head_specs(),
        out_shape=[
            jax.ShapeDtypeStruct((1, TOK, groups * part), BF16)
            for part in (HEADS * HEAD, HEAD, HEAD)
        ],
        cost_estimate=pl.CostEstimate(flops=0, bytes_accessed=4 * packed.size, transcendentals=0),
        name="unpack",
    )(packed)


def upstream_kernel(ids_ref, *refs):
    pieces, (w_ref, o_ref, acc_ref) = refs[:-3], refs[-3:]
    step = pl.program_id(0)
    rows = jnp.concatenate([piece[...] for piece in pieces], 0)
    part = jnp.dot(rows, w_ref[...], preferred_element_type=F32)

    @pl.when(step == 0)
    def _():
        acc_ref[...] = part

    @pl.when(step > 0)
    def _():
        acc_ref[...] += part

    @pl.when(step == pl.num_programs(0) - 1)
    def _():
        for p in range(len(pieces)):
            o_ref[ids_ref[p]] = acc_ref[p * TOK : (p + 1) * TOK, :].astype(BF16)


def upstream(ids, pieces, weight):
    depth, width = weight.shape
    chunk = 512
    count = len(pieces)
    return pl.pallas_call(
        upstream_kernel,
        grid_spec=pltpu.PrefetchScalarGridSpec(
            num_scalar_prefetch=1,
            grid=(depth // chunk,),
            in_specs=[pl.BlockSpec((TOK, chunk), lambda i, ids: (0, i))] * count
            + [pl.BlockSpec((chunk, width), lambda i, ids: (i, 0))],
            out_specs=pl.BlockSpec((count, TOK, width), lambda i, ids: (0, 0, 0)),
            scratch_shapes=[pltpu.VMEM((count * TOK, width), F32)],
        ),
        out_shape=jax.ShapeDtypeStruct((count, TOK, width), BF16),
        cost_estimate=pl.CostEstimate(
            flops=2 * count * TOK * width * depth,
            bytes_accessed=2 * (count * TOK * (depth + width) + depth * width),
            transcendentals=0,
        ),
        name="upstream",
    )(ids, *pieces, weight)


def proj_kernel(ids_ref, *refs):
    pieces, (ot_ref, a_ref, b_ref, lhs_ref) = refs[:-4], refs[-4:]
    count = len(pieces)
    near = a_ref.shape[0]
    half = a_ref.shape[2]

    @pl.when(pl.program_id(0) == 0)
    def _():
        for p in range(count):
            lhs_ref[:, p * TOK : (p + 1) * TOK] = ot_ref[ids_ref[p]]

    rows = jnp.concatenate([piece[...] for piece in pieces], 0)
    out = jnp.dot(lhs_ref[...], rows, preferred_element_type=F32).astype(BF16)
    for t in range(near):
        part = out[:, t * TOK : (t + 1) * TOK]
        a_ref[lax.rem(t + near - ids_ref[count + 1], near), 0] = part[:half]
        b_ref[0, t] = part[half:]


def proj_terms(ids, pieces, ot):
    count, width, _ = ot.shape
    far, near = GRID["dp"], GRID["fsdp"]
    half = width // 2
    depth = pieces[0].shape[1]

    def place(i, ids):
        return lax.rem(ids[count] + i, far)

    return pl.pallas_call(
        proj_kernel,
        grid_spec=pltpu.PrefetchScalarGridSpec(
            num_scalar_prefetch=1,
            grid=(far,),
            in_specs=[pl.BlockSpec((TOK, near * TOK), lambda i, ids: (0, place(i, ids)))] * count
            + [pl.BlockSpec(ot.shape, lambda i, ids: (0, 0, 0))],
            out_specs=[
                pl.BlockSpec((near, 1, half, TOK), lambda i, ids: (0, place(i, ids), 0, 0)),
                pl.BlockSpec((1, near, half, TOK), lambda i, ids: (i, 0, 0, 0)),
            ],
            scratch_shapes=[pltpu.VMEM((width, count * TOK), BF16)],
        ),
        out_shape=[
            jax.ShapeDtypeStruct((near, far, half, TOK), BF16),
            jax.ShapeDtypeStruct((far, near, half, TOK), BF16),
        ],
        cost_estimate=pl.CostEstimate(
            flops=2 * count * TOK * width * depth,
            bytes_accessed=2 * (count * TOK * (depth + width) + depth * width),
            transcendentals=0,
        ),
        name="proj_terms",
    )(ids, *pieces, ot)


def shift(x, axis, by):
    n = GRID[axis]
    return lax.ppermute(x, axis, [(i, (i + by) % n) for i in range(n)])


def add(a, b):
    return (a.astype(F32) + b.astype(F32)).astype(BF16)


def ring_sum(terms, axis):
    n = GRID[axis]
    far = n // 2
    m = terms.shape[1] // 2
    up = shift(terms[far, :m], axis, 1)
    down = shift(terms[far, m:], axis, -1)
    up = jnp.concatenate([add(terms[far - 1, :m], up), terms[far - 1, m:]], 0)
    down = jnp.concatenate([terms[n - far + 1, :m], add(terms[n - far + 1, m:], down)], 0)
    for k in range(far - 1, 0, -1):
        up = shift(up, axis, 1)
        down = shift(down, axis, -1)
        if k > 1:
            up = add(terms[k - 1], up)
            down = add(terms[n - k + 1], down)
    return (terms[0].astype(F32) + up.astype(F32) + down.astype(F32)).astype(BF16)


def swap(x, axis):
    return lax.all_to_all(x, axis, split_axis=0, concat_axis=0, tiled=True)


def hop(x, chips, core):
    pairs = [(i * 2 + c, ((i + chips) % 4) * 2 + (c ^ core)) for i in range(4) for c in range(2)]
    return lax.ppermute(x, "seq", pairs)


def gather_tokens(own):
    m = own.shape[0] // 2
    left = hop(own, 1, 0)
    right = hop(own, -1, 0)
    across = jnp.concatenate([hop(left[:m], 1, 0), hop(right[m:], -1, 0)], 0)
    mine = [own, left, right, across]
    return mine + [hop(piece, 0, 1) for piece in mine]


def per_device(
    query_rows, forward_key_rows, forward_value_rows, out_cotangent, proj_weight, sent_lengths
):
    place = lax.axis_index("seq").astype(jnp.int32)
    chip, core = place // 2, place % 2
    offsets = jnp.array([0, 3, 1, 2], jnp.int32)
    chips = (chip + offsets) % 4 * 2
    ids = jnp.concatenate(
        [
            chips + core,
            chips + 1 - core,
            jnp.stack([lax.axis_index("dp"), lax.axis_index("fsdp")]).astype(jnp.int32),
        ]
    )
    weight = lax.all_gather(proj_weight, ("dp", "fsdp"), axis=0, tiled=True)
    packed = swap(pack(query_rows, forward_key_rows, forward_value_rows), "seq")
    pieces = gather_tokens(out_cotangent[0])
    lo, hi = limits(sent_lengths[0], packed.shape[0])
    output = attend(packed, lo, hi)
    first, second = proj_terms(ids, pieces, output)
    first = ring_sum(first, "fsdp")
    second = ring_sum(second, "dp")
    grads = attend_grad(packed, upstream(ids, pieces, weight), lo, hi)
    first = jnp.sum(swap(first, "dp").astype(F32), axis=0)
    second = jnp.sum(swap(second, "fsdp").astype(F32), axis=0)
    proj_grad = jnp.concatenate([first, second], 0).T.astype(BF16)
    query_grad, key_gradient, value_gradient = unpack(swap(grads, "seq"))
    return (query_grad, key_gradient, value_gradient, proj_grad)


def solution(mesh):
    in_specs = (
        P(("dp", "fsdp"), "seq", None),
        P(("dp", "fsdp"), "seq", None),
        P(("dp", "fsdp"), "seq", None),
        P(("dp", "fsdp"), "seq", None),
        P(("dp", "fsdp"), "seq"),
        P(("dp", "fsdp"), None),
    )
    out_specs = (
        P(("dp", "fsdp"), "seq", None),
        P(("dp", "fsdp"), "seq", None),
        P(("dp", "fsdp"), "seq", None),
        P(("dp", "fsdp"), "seq"),
    )
    return jax.shard_map(
        per_device, mesh=mesh, in_specs=in_specs, out_specs=out_specs, check_vma=False
    )
```

```python
import math

import jax
import jax.numpy as jnp
from jax import lax
from jax.experimental import pallas as pl
from jax.experimental.pallas import tpu as pltpu
from jax.sharding import PartitionSpec as P

HEADS = 4
HEAD = 128
TOK = 128
KW = 448
FACTOR = 1.0 / math.sqrt(HEAD)
F32 = jnp.float32
BF16 = jnp.bfloat16
GROUP = 4
GRID = {"dp": 8, "fsdp": 4}


def window_start(i, blocks):
    return pl.multiple_of(jnp.clip(i * TOK - 256, 0, blocks * TOK - KW), 64)


def probs(i, start, g_ref, lo_ref, hi_ref, key, h0):
    q = jnp.concatenate(
        [g_ref[i, :, (h0 + j) * HEAD : (h0 + j + 1) * HEAD] for j in range(GROUP)], 0
    )
    s = lax.dot_general(key, q, (((1,), (1,)), ((), ())), preferred_element_type=F32)
    place = start + lax.broadcasted_iota(jnp.int32, (KW, GROUP * TOK), 0)
    lo = jnp.concatenate([lo_ref[i]] * GROUP, 1)
    hi = jnp.concatenate([hi_ref[i]] * GROUP, 1)
    p = jnp.where((place >= lo) & (place < hi), jnp.exp(s * FACTOR), 0.0)
    a = p * (1.0 / jnp.sum(p, axis=0, keepdims=True))
    return q, a


def unpack_keys(g_ref, k_ref, v_ref):
    for b in range(g_ref.shape[0]):
        rows = slice(b * TOK, (b + 1) * TOK)
        k_ref[rows, :] = g_ref[b, :, HEADS * HEAD : (HEADS + 1) * HEAD]
        v_ref[rows, :] = g_ref[b, :, (HEADS + 1) * HEAD :]


def fwd_kernel(g_ref, lo_ref, hi_ref, o_ref, k_ref, v_ref):
    blocks = g_ref.shape[0]
    i = pl.program_id(0)

    @pl.when(i == 0)
    def _():
        unpack_keys(g_ref, k_ref, v_ref)

    start = window_start(i, blocks)
    key = k_ref[pl.ds(start, KW), :]
    vt = v_ref[pl.ds(start, KW), :].T
    for h0 in range(0, HEADS, GROUP):
        _, a = probs(i, start, g_ref, lo_ref, hi_ref, key, h0)
        o = jnp.dot(vt, a.astype(BF16), preferred_element_type=F32).astype(BF16)
        for j in range(GROUP):
            o_ref[0, (h0 + j) * HEAD : (h0 + j + 1) * HEAD, :] = o[:, j * TOK : (j + 1) * TOK]


def bwd_kernel(g_ref, u_ref, lo_ref, hi_ref, o_ref, dk_ref, dv_ref, k_ref, v_ref):
    blocks = g_ref.shape[0]
    i = pl.program_id(0)

    @pl.when(i == 0)
    def _():
        unpack_keys(g_ref, k_ref, v_ref)
        dk_ref[...] = jnp.zeros_like(dk_ref)
        dv_ref[...] = jnp.zeros_like(dv_ref)

    start = window_start(i, blocks)
    key = k_ref[pl.ds(start, KW), :]
    val = v_ref[pl.ds(start, KW), :]
    kt = key.T
    dk = None
    for h0 in range(0, HEADS, GROUP):
        q, a = probs(i, start, g_ref, lo_ref, hi_ref, key, h0)
        u = jnp.concatenate(
            [u_ref[i, :, (h0 + j) * HEAD : (h0 + j + 1) * HEAD] for j in range(GROUP)], 0
        )
        g = lax.dot_general(val, u, (((1,), (1,)), ((), ())), preferred_element_type=F32)
        delta = jnp.sum(a * g, axis=0, keepdims=True)
        ds = (a * (g - delta) * FACTOR).astype(BF16)
        dq = jnp.dot(kt, ds, preferred_element_type=F32)
        for j in range(GROUP):
            o_ref[i, :, (h0 + j) * HEAD : (h0 + j + 1) * HEAD] = dq[
                :, j * TOK : (j + 1) * TOK
            ].T.astype(BF16)
        dkh = jnp.dot(ds, q, preferred_element_type=F32)
        dvh = jnp.dot(a.astype(BF16), u, preferred_element_type=F32)
        dk, dv = (dkh, dvh) if dk is None else (dk + dkh, dv + dvh)
    dk_ref[pl.ds(start, KW), :] += dk
    dv_ref[pl.ds(start, KW), :] += dv

    @pl.when(i == blocks - 1)
    def _():
        for b in range(blocks):
            o_ref[b, :, HEADS * HEAD : (HEADS + 1) * HEAD] = dk_ref[
                b * TOK : (b + 1) * TOK, :
            ].astype(BF16)
            o_ref[b, :, (HEADS + 1) * HEAD :] = dv_ref[b * TOK : (b + 1) * TOK, :].astype(BF16)


def whole(shape):
    return pl.BlockSpec(shape, lambda i: (0,) * len(shape))


def limits(sent_lengths, blocks):
    number = sent_lengths.shape[0]
    order = jnp.arange(number, dtype=jnp.int32)
    ends = jnp.sum(jnp.where(order[None, :] <= order[:, None], sent_lengths[None, :], 0), axis=1)
    places = jnp.arange(blocks * TOK, dtype=jnp.int32)
    sentence = jnp.sum((places[:, None] >= ends[None, :]).astype(jnp.int32), axis=1)
    lo = jnp.sum(
        jnp.where(order[None, :] + 3 < sentence[:, None], sent_lengths[None, :], 0), axis=1
    )
    hi = jnp.sum(jnp.where(order[None, :] <= sentence[:, None], sent_lengths[None, :], 0), axis=1)
    return lo.reshape(blocks, 1, TOK), hi.reshape(blocks, 1, TOK)


def attend(g, lo, hi):
    blocks = g.shape[0]
    pairs = blocks * TOK * KW * HEADS
    return pl.pallas_call(
        fwd_kernel,
        grid=(blocks,),
        in_specs=[whole(x.shape) for x in (g, lo, hi)],
        out_specs=pl.BlockSpec((1, HEADS * HEAD, TOK), lambda i: (i, 0, 0)),
        out_shape=jax.ShapeDtypeStruct((blocks, HEADS * HEAD, TOK), BF16),
        scratch_shapes=[pltpu.VMEM((blocks * TOK, HEAD), BF16)] * 2,
        cost_estimate=pl.CostEstimate(
            flops=4 * pairs * HEAD, bytes_accessed=4 * g.size, transcendentals=pairs
        ),
        name="attend",
    )(g, lo, hi)


def attend_grad(g, u, lo, hi):
    blocks = g.shape[0]
    pairs = blocks * TOK * KW * HEADS
    return pl.pallas_call(
        bwd_kernel,
        grid=(blocks,),
        in_specs=[whole(x.shape) for x in (g, u, lo, hi)],
        out_specs=whole(g.shape),
        out_shape=jax.ShapeDtypeStruct(g.shape, BF16),
        scratch_shapes=[pltpu.VMEM((blocks * TOK, HEAD), F32)] * 2
        + [pltpu.VMEM((blocks * TOK, HEAD), BF16)] * 2,
        cost_estimate=pl.CostEstimate(
            flops=10 * pairs * HEAD, bytes_accessed=6 * g.size, transcendentals=pairs
        ),
        name="attend_grad",
    )(g, u, lo, hi)


def head_parts(g):
    wide = HEADS * HEAD
    return (
        (slice(0, wide), slice(g * wide, (g + 1) * wide)),
        (slice(wide, wide + HEAD), slice(g * HEAD, (g + 1) * HEAD)),
        (slice(wide + HEAD, wide + 2 * HEAD), slice(g * HEAD, (g + 1) * HEAD)),
    )


def pack_kernel(q_ref, k_ref, v_ref, o_ref):
    for g in range(o_ref.shape[0]):
        for ref, (inner, outer) in zip((q_ref, k_ref, v_ref), head_parts(g)):
            o_ref[g, :, inner] = ref[0, :, outer]


def pack(q, k, v):
    groups = k.shape[2] // HEAD
    return pl.pallas_call(
        pack_kernel,
        out_shape=jax.ShapeDtypeStruct((groups, TOK, (HEADS + 2) * HEAD), BF16),
        cost_estimate=pl.CostEstimate(flops=0, bytes_accessed=6 * q.size, transcendentals=0),
        name="pack",
    )(q, k, v)


def unpack_kernel(i_ref, q_ref, k_ref, v_ref):
    for g in range(i_ref.shape[0]):
        for ref, (inner, outer) in zip((q_ref, k_ref, v_ref), head_parts(g)):
            ref[0, :, outer] = i_ref[g, :, inner]


def unpack(packed):
    groups = packed.shape[0]
    return pl.pallas_call(
        unpack_kernel,
        out_shape=[
            jax.ShapeDtypeStruct((1, TOK, groups * part), BF16)
            for part in (HEADS * HEAD, HEAD, HEAD)
        ],
        cost_estimate=pl.CostEstimate(flops=0, bytes_accessed=4 * packed.size, transcendentals=0),
        name="unpack",
    )(packed)


def upstream_kernel(ids_ref, *refs):
    pieces, weights, (o_ref, acc_ref, w_ref) = refs[:-8], refs[-8:-3], refs[-3:]
    count = len(pieces)
    near = w_ref.shape[1]
    step = pl.program_id(0)
    last = pl.num_programs(0) - 1
    y = ids_ref[count + 1]
    mine, below, above, far_low, far_high = weights
    w_ref[:, y] = mine[...]
    w_ref[:, lax.rem(y + near - 1, near)] = below[...]
    w_ref[:, lax.rem(y + 1, near)] = above[...]

    @pl.when(step * 2 <= last)
    def _():
        w_ref[:, lax.rem(y + 2, near)] = far_low[...]

    @pl.when(step * 2 > last)
    def _():
        w_ref[:, lax.rem(y + 2, near)] = far_high[...]

    rows = jnp.concatenate([piece[...] for piece in pieces], 0)
    weight = w_ref[...].reshape(rows.shape[1], w_ref.shape[3])
    part = jnp.dot(rows, weight, preferred_element_type=F32)

    @pl.when(step == 0)
    def _():
        acc_ref[...] = part

    @pl.when(step > 0)
    def _():
        acc_ref[...] += part

    @pl.when(step == last)
    def _():
        for p in range(count):
            o_ref[ids_ref[p]] = acc_ref[p * TOK : (p + 1) * TOK, :].astype(BF16)


def upstream(ids, pieces, weights):
    far, rows, width = weights[0].shape
    near = GRID["fsdp"]
    depth = far * near * rows
    planes = 2
    steps = far // planes
    count = len(pieces)
    block = (planes, rows, width)
    return pl.pallas_call(
        upstream_kernel,
        grid_spec=pltpu.PrefetchScalarGridSpec(
            num_scalar_prefetch=1,
            grid=(steps,),
            in_specs=[pl.BlockSpec((TOK, depth // steps), lambda i, ids: (0, i))] * count
            + [pl.BlockSpec(block, lambda i, ids: (i, 0, 0))] * 3
            + [
                pl.BlockSpec(block, lambda i, ids: (jnp.minimum(i, steps // 2 - 1), 0, 0)),
                pl.BlockSpec(block, lambda i, ids: (jnp.maximum(i - steps // 2, 0), 0, 0)),
            ],
            out_specs=pl.BlockSpec((count, TOK, width), lambda i, ids: (0, 0, 0)),
            scratch_shapes=[
                pltpu.VMEM((count * TOK, width), F32),
                pltpu.VMEM((planes, near, rows, width), BF16),
            ],
        ),
        out_shape=jax.ShapeDtypeStruct((count, TOK, width), BF16),
        cost_estimate=pl.CostEstimate(
            flops=2 * count * TOK * width * depth,
            bytes_accessed=2 * (count * TOK * (depth + width) + depth * width),
            transcendentals=0,
        ),
        name="upstream",
    )(ids, *pieces, *weights)


def proj_kernel(ids_ref, *refs):
    pieces, (ot_ref, a_ref, b_ref, lhs_ref) = refs[:-4], refs[-4:]
    count = len(pieces)
    near = a_ref.shape[0]
    split = a_ref.shape[2]

    @pl.when(pl.program_id(0) == 0)
    def _():
        for p in range(count):
            lhs_ref[:, p * TOK : (p + 1) * TOK] = ot_ref[ids_ref[p]]

    rows = jnp.concatenate([piece[...] for piece in pieces], 0)
    out = jnp.dot(lhs_ref[...], rows, preferred_element_type=F32).astype(BF16)
    for t in range(near):
        part = out[:, t * TOK : (t + 1) * TOK]
        a_ref[lax.rem(t + near - ids_ref[count + 1], near), 0] = part[:split]
        b_ref[0, t] = part[split:]


def proj_terms(ids, pieces, ot):
    count, width, _ = ot.shape
    far, near = GRID["dp"], GRID["fsdp"]
    split = width * 3 // 4
    depth = pieces[0].shape[1]

    return pl.pallas_call(
        proj_kernel,
        grid_spec=pltpu.PrefetchScalarGridSpec(
            num_scalar_prefetch=1,
            grid=(far,),
            in_specs=[pl.BlockSpec((TOK, near * TOK), lambda i, ids: (0, i))] * count
            + [pl.BlockSpec(ot.shape, lambda i, ids: (0, 0, 0))],
            out_specs=[
                pl.BlockSpec((near, 1, split, TOK), lambda i, ids: (0, lax.rem(i + far - ids[count], far), 0, 0)),
                pl.BlockSpec((1, near, width - split, TOK), lambda i, ids: (i, 0, 0, 0)),
            ],
            scratch_shapes=[pltpu.VMEM((width, count * TOK), BF16)],
        ),
        out_shape=[
            jax.ShapeDtypeStruct((near, far, split, TOK), BF16),
            jax.ShapeDtypeStruct((far, near, width - split, TOK), BF16),
        ],
        cost_estimate=pl.CostEstimate(
            flops=2 * count * TOK * width * depth,
            bytes_accessed=2 * (count * TOK * (depth + width) + depth * width),
            transcendentals=0,
        ),
        name="proj_terms",
    )(ids, *pieces, ot)


def shift(x, axis, by):
    n = GRID[axis]
    return lax.ppermute(x, axis, [(i, (i + by) % n) for i in range(n)])


def add(a, b):
    return (a.astype(F32) + b.astype(F32)).astype(BF16)


def after(value, done):
    return lax.optimization_barrier((value, done))[0]


def swap(x, axis):
    return lax.all_to_all(x, axis, split_axis=0, concat_axis=0, tiled=True)


def hop(x, chips, core):
    pairs = [(i * 2 + c, ((i + chips) % 4) * 2 + (c ^ core)) for i in range(4) for c in range(2)]
    return lax.ppermute(x, "seq", pairs)


def per_device(
    query_rows, forward_key_rows, forward_value_rows, out_cotangent, proj_weight, sent_lengths
):
    place = lax.axis_index("seq").astype(jnp.int32)
    chip, core = place // 2, place % 2
    offsets = jnp.array([0, 3, 1, 2], jnp.int32)
    chips = (chip + offsets) % 4 * 2
    ids = jnp.concatenate(
        [
            chips + core,
            chips + 1 - core,
            jnp.stack([lax.axis_index("dp"), lax.axis_index("fsdp")]).astype(jnp.int32),
        ]
    )
    far = GRID["dp"] // 2
    half = TOK // 2
    own = out_cotangent[0]
    weight = jnp.broadcast_to(proj_weight, (2 * far, *proj_weight.shape))
    weight = swap(weight, "dp")
    left, right = hop(own, 1, 0), hop(own, -1, 0)
    local = pack(query_rows, forward_key_rows, forward_value_rows)
    partner = hop(own, 0, 1)
    packed = swap(local, "seq")
    below, above = shift(weight, "fsdp", 1), shift(weight, "fsdp", -1)
    lo, hi = limits(sent_lengths[0], packed.shape[0])
    across = [hop(left[:half], 1, 0), hop(right[half:], -1, 0)]
    across = jnp.concatenate(across, 0)
    output = attend(packed, lo, hi)
    pieces = [own, left, right, across, partner]
    pieces += [hop(piece, 0, 1) for piece in (left, right, across)]
    ends = [shift(below[:far], "fsdp", 1), shift(above[far:], "fsdp", -1)]
    first, second = proj_terms(ids, pieces, output)
    second = swap(second, "dp")
    up, down = shift(first[2, :far], "fsdp", 1), shift(first[2, far:], "fsdp", -1)
    arriving = upstream(ids, pieces, [weight, below, above, *ends])
    up, down = after((up, down), arriving)
    up = shift(jnp.concatenate([add(first[1, :far], up), first[1, far:]], 0), "fsdp", 1)
    down = shift(jnp.concatenate([first[3, :far], add(first[3, far:], down)], 0), "fsdp", -1)
    grads = attend_grad(packed, arriving, lo, hi)
    grads_home = swap(grads, "seq")
    up, down, second = after((up, down, second), grads)
    first = (first[0].astype(F32) + up.astype(F32) + down.astype(F32)).astype(BF16)
    part = first.shape[1] // 2
    up, down = shift(first[4, :part], "dp", 1), shift(first[4, part:], "dp", -1)
    up = jnp.concatenate([add(first[3, :part], up), first[3, part:]], 0)
    down = jnp.concatenate([first[5, :part], add(first[5, part:], down)], 0)
    up, down = shift(up, "dp", 1), shift(down, "dp", -1)
    up, down = add(first[2], up), add(first[6], down)
    up, down = shift(up, "dp", 1), shift(down, "dp", -1)
    up, down = add(first[1], up), add(first[7], down)
    up, down = shift(up, "dp", 1), shift(down, "dp", -1)
    second = jnp.sum(second.astype(F32), axis=0).astype(BF16)
    second = swap(second, "fsdp")
    first = first[0].astype(F32) + up.astype(F32) + down.astype(F32)
    proj_grad = jnp.concatenate([first, jnp.sum(second.astype(F32), axis=0)], 0)
    query_grad, key_gradient, value_gradient = unpack(grads_home)
    return (query_grad, key_gradient, value_gradient, proj_grad.T.astype(BF16))


def solution(mesh):
    in_specs = (
        P(("dp", "fsdp"), "seq", None),
        P(("dp", "fsdp"), "seq", None),
        P(("dp", "fsdp"), "seq", None),
        P(("dp", "fsdp"), "seq", None),
        P(("dp", "fsdp"), "seq"),
        P(("dp", "fsdp"), None),
    )
    out_specs = (
        P(("dp", "fsdp"), "seq", None),
        P(("dp", "fsdp"), "seq", None),
        P(("dp", "fsdp"), "seq", None),
        P(("dp", "fsdp"), "seq"),
    )
    return jax.shard_map(
        per_device, mesh=mesh, in_specs=in_specs, out_specs=out_specs, check_vma=False
    )
```

```python
import math

import jax
import jax.numpy as jnp
from jax import lax
from jax.experimental import pallas as pl
from jax.experimental.pallas import tpu as pltpu
from jax.sharding import PartitionSpec as P

HEADS = 4
HEAD = 128
TOK = 128
KW = 448
FACTOR = 1.0 / math.sqrt(HEAD)
F32 = jnp.float32
BF16 = jnp.bfloat16
GROUP = 4
GRID = {"dp": 8, "fsdp": 4}


def window_start(i, blocks):
    return pl.multiple_of(jnp.clip(i * TOK - 256, 0, blocks * TOK - KW), 64)


def probs(i, start, q_ref, lo_ref, hi_ref, key, h0):
    q = jnp.concatenate(
        [q_ref[i, :, (h0 + j) * HEAD : (h0 + j + 1) * HEAD] for j in range(GROUP)], 0
    )
    s = lax.dot_general(key, q, (((1,), (1,)), ((), ())), preferred_element_type=F32)
    place = start + lax.broadcasted_iota(jnp.int32, (KW, GROUP * TOK), 0)
    lo = jnp.concatenate([lo_ref[i]] * GROUP, 1)
    hi = jnp.concatenate([hi_ref[i]] * GROUP, 1)
    p = jnp.where((place >= lo) & (place < hi), jnp.exp(s * FACTOR), 0.0)
    a = p * (1.0 / jnp.sum(p, axis=0, keepdims=True))
    return q, a


def assemble(ids_ref, pieces, q_ref, k_ref, v_ref):
    for p, piece in enumerate(pieces):
        b = ids_ref[p]
        rows = pl.ds(pl.multiple_of(b * TOK, TOK), TOK)
        q_ref[b] = piece[:, : HEADS * HEAD]
        k_ref[rows, :] = piece[:, HEADS * HEAD : (HEADS + 1) * HEAD]
        v_ref[rows, :] = piece[:, (HEADS + 1) * HEAD :]


def fwd_kernel(ids_ref, *refs):
    pieces, (lo_ref, hi_ref, o_ref, q_ref, k_ref, v_ref) = refs[:-6], refs[-6:]
    blocks = len(pieces)
    i = pl.program_id(0)

    @pl.when(i == 0)
    def _():
        assemble(ids_ref, pieces, q_ref, k_ref, v_ref)

    start = window_start(i, blocks)
    key = k_ref[pl.ds(start, KW), :]
    vt = v_ref[pl.ds(start, KW), :].T
    for h0 in range(0, HEADS, GROUP):
        _, a = probs(i, start, q_ref, lo_ref, hi_ref, key, h0)
        o = jnp.dot(vt, a.astype(BF16), preferred_element_type=F32).astype(BF16)
        for j in range(GROUP):
            o_ref[0, (h0 + j) * HEAD : (h0 + j + 1) * HEAD, :] = o[:, j * TOK : (j + 1) * TOK]


def bwd_kernel(ids_ref, *refs):
    pieces, refs = refs[:-9], refs[-9:]
    u_ref, lo_ref, hi_ref, o_ref, dk_ref, dv_ref, q_ref, k_ref, v_ref = refs
    blocks = len(pieces)
    i = pl.program_id(0)

    @pl.when(i == 0)
    def _():
        assemble(ids_ref, pieces, q_ref, k_ref, v_ref)
        dk_ref[...] = jnp.zeros_like(dk_ref)
        dv_ref[...] = jnp.zeros_like(dv_ref)

    start = window_start(i, blocks)
    key = k_ref[pl.ds(start, KW), :]
    val = v_ref[pl.ds(start, KW), :]
    kt = key.T
    dk = None
    for h0 in range(0, HEADS, GROUP):
        q, a = probs(i, start, q_ref, lo_ref, hi_ref, key, h0)
        u = jnp.concatenate(
            [u_ref[i, :, (h0 + j) * HEAD : (h0 + j + 1) * HEAD] for j in range(GROUP)], 0
        )
        g = lax.dot_general(val, u, (((1,), (1,)), ((), ())), preferred_element_type=F32)
        delta = jnp.sum(a * g, axis=0, keepdims=True)
        ds = (a * (g - delta) * FACTOR).astype(BF16)
        dq = jnp.dot(kt, ds, preferred_element_type=F32)
        for j in range(GROUP):
            o_ref[i, :, (h0 + j) * HEAD : (h0 + j + 1) * HEAD] = dq[
                :, j * TOK : (j + 1) * TOK
            ].T.astype(BF16)
        dkh = jnp.dot(ds, q, preferred_element_type=F32)
        dvh = jnp.dot(a.astype(BF16), u, preferred_element_type=F32)
        dk, dv = (dkh, dvh) if dk is None else (dk + dkh, dv + dvh)
    dk_ref[pl.ds(start, KW), :] += dk
    dv_ref[pl.ds(start, KW), :] += dv

    @pl.when(i == blocks - 1)
    def _():
        for b in range(blocks):
            o_ref[b, :, HEADS * HEAD : (HEADS + 1) * HEAD] = dk_ref[
                b * TOK : (b + 1) * TOK, :
            ].astype(BF16)
            o_ref[b, :, (HEADS + 1) * HEAD :] = dv_ref[b * TOK : (b + 1) * TOK, :].astype(BF16)


def whole(shape):
    return pl.BlockSpec(shape, lambda i, ids: (0,) * len(shape))


def limits(sent_lengths, blocks):
    number = sent_lengths.shape[0]
    order = jnp.arange(number, dtype=jnp.int32)
    ends = jnp.sum(jnp.where(order[None, :] <= order[:, None], sent_lengths[None, :], 0), axis=1)
    places = jnp.arange(blocks * TOK, dtype=jnp.int32)
    sentence = jnp.sum((places[:, None] >= ends[None, :]).astype(jnp.int32), axis=1)
    lo = jnp.sum(
        jnp.where(order[None, :] + 3 < sentence[:, None], sent_lengths[None, :], 0), axis=1
    )
    hi = jnp.sum(jnp.where(order[None, :] <= sentence[:, None], sent_lengths[None, :], 0), axis=1)
    return lo.reshape(blocks, 1, TOK), hi.reshape(blocks, 1, TOK)


def head_scratch(blocks):
    keys = pltpu.VMEM((blocks * TOK, HEAD), BF16)
    return [pltpu.VMEM((blocks, TOK, HEADS * HEAD), BF16), keys, keys]


def attend(ids, pieces, lo, hi):
    blocks = len(pieces)
    pairs = blocks * TOK * KW * HEADS
    return pl.pallas_call(
        fwd_kernel,
        grid_spec=pltpu.PrefetchScalarGridSpec(
            num_scalar_prefetch=1,
            grid=(blocks,),
            in_specs=[whole(x.shape) for x in (*pieces, lo, hi)],
            out_specs=pl.BlockSpec((1, HEADS * HEAD, TOK), lambda i, ids: (i, 0, 0)),
            scratch_shapes=head_scratch(blocks),
        ),
        out_shape=jax.ShapeDtypeStruct((blocks, HEADS * HEAD, TOK), BF16),
        cost_estimate=pl.CostEstimate(
            flops=4 * pairs * HEAD,
            bytes_accessed=4 * blocks * pieces[0].size,
            transcendentals=pairs,
        ),
        name="attend",
    )(ids, *pieces, lo, hi)


def attend_grad(ids, pieces, u, lo, hi):
    blocks = len(pieces)
    pairs = blocks * TOK * KW * HEADS
    shape = (blocks, *pieces[0].shape)
    return pl.pallas_call(
        bwd_kernel,
        grid_spec=pltpu.PrefetchScalarGridSpec(
            num_scalar_prefetch=1,
            grid=(blocks,),
            in_specs=[whole(x.shape) for x in (*pieces, u, lo, hi)],
            out_specs=whole(shape),
            scratch_shapes=[pltpu.VMEM((blocks * TOK, HEAD), F32)] * 2 + head_scratch(blocks),
        ),
        out_shape=jax.ShapeDtypeStruct(shape, BF16),
        cost_estimate=pl.CostEstimate(
            flops=10 * pairs * HEAD,
            bytes_accessed=6 * blocks * pieces[0].size,
            transcendentals=pairs,
        ),
        name="attend_grad",
    )(ids, *pieces, u, lo, hi)


def head_parts(g):
    wide = HEADS * HEAD
    return (
        (slice(0, wide), slice(g * wide, (g + 1) * wide)),
        (slice(wide, wide + HEAD), slice(g * HEAD, (g + 1) * HEAD)),
        (slice(wide + HEAD, wide + 2 * HEAD), slice(g * HEAD, (g + 1) * HEAD)),
    )


def pack_kernel(ids_ref, q_ref, k_ref, v_ref, *o_refs):
    wide = HEADS * HEAD
    for p, o_ref in enumerate(o_refs):
        g = ids_ref[p]
        heads = pl.ds(pl.multiple_of(g * HEAD, HEAD), HEAD)
        o_ref[:, :wide] = q_ref[0, :, pl.ds(pl.multiple_of(g * wide, wide), wide)]
        o_ref[:, wide : wide + HEAD] = k_ref[0, :, heads]
        o_ref[:, wide + HEAD :] = v_ref[0, :, heads]


def pack(ids, q, k, v):
    groups = k.shape[2] // HEAD
    width = (HEADS + 2) * HEAD
    return pl.pallas_call(
        pack_kernel,
        grid_spec=pltpu.PrefetchScalarGridSpec(
            num_scalar_prefetch=1,
            grid=(1,),
            in_specs=[whole(x.shape) for x in (q, k, v)],
            out_specs=[whole((TOK, width))] * groups,
        ),
        out_shape=[jax.ShapeDtypeStruct((TOK, width), BF16)] * groups,
        cost_estimate=pl.CostEstimate(flops=0, bytes_accessed=6 * q.size, transcendentals=0),
        name="pack",
    )(ids, q, k, v)


def unpack_kernel(i_ref, q_ref, k_ref, v_ref):
    for g in range(i_ref.shape[0]):
        for ref, (inner, outer) in zip((q_ref, k_ref, v_ref), head_parts(g)):
            ref[0, :, outer] = i_ref[g, :, inner]


def unpack(packed):
    groups = packed.shape[0]
    return pl.pallas_call(
        unpack_kernel,
        out_shape=[
            jax.ShapeDtypeStruct((1, TOK, groups * part), BF16)
            for part in (HEADS * HEAD, HEAD, HEAD)
        ],
        cost_estimate=pl.CostEstimate(flops=0, bytes_accessed=4 * packed.size, transcendentals=0),
        name="unpack",
    )(packed)


def upstream_kernel(ids_ref, *refs):
    pieces, weights, (o_ref, acc_ref, w_ref) = refs[:-8], refs[-8:-3], refs[-3:]
    count = len(pieces)
    near = w_ref.shape[1]
    step = pl.program_id(0)
    last = pl.num_programs(0) - 1
    y = ids_ref[count + 1]
    mine, below, above, far_low, far_high = weights
    w_ref[:, y] = mine[...]
    w_ref[:, lax.rem(y + near - 1, near)] = below[...]
    w_ref[:, lax.rem(y + 1, near)] = above[...]

    @pl.when(step * 2 <= last)
    def _():
        w_ref[:, lax.rem(y + 2, near)] = far_low[...]

    @pl.when(step * 2 > last)
    def _():
        w_ref[:, lax.rem(y + 2, near)] = far_high[...]

    rows = jnp.concatenate([piece[...] for piece in pieces], 0)
    weight = w_ref[...].reshape(rows.shape[1], w_ref.shape[3])
    part = jnp.dot(rows, weight, preferred_element_type=F32)

    @pl.when(step == 0)
    def _():
        acc_ref[...] = part

    @pl.when(step > 0)
    def _():
        acc_ref[...] += part

    @pl.when(step == last)
    def _():
        for p in range(count):
            o_ref[ids_ref[p]] = acc_ref[p * TOK : (p + 1) * TOK, :].astype(BF16)


def upstream(ids, pieces, weights):
    far, rows, width = weights[0].shape
    near = GRID["fsdp"]
    depth = far * near * rows
    planes = 2
    steps = far // planes
    count = len(pieces)
    block = (planes, rows, width)
    return pl.pallas_call(
        upstream_kernel,
        grid_spec=pltpu.PrefetchScalarGridSpec(
            num_scalar_prefetch=1,
            grid=(steps,),
            in_specs=[pl.BlockSpec((TOK, depth // steps), lambda i, ids: (0, i))] * count
            + [pl.BlockSpec(block, lambda i, ids: (i, 0, 0))] * 3
            + [
                pl.BlockSpec(block, lambda i, ids: (jnp.minimum(i, steps // 2 - 1), 0, 0)),
                pl.BlockSpec(block, lambda i, ids: (jnp.maximum(i - steps // 2, 0), 0, 0)),
            ],
            out_specs=pl.BlockSpec((count, TOK, width), lambda i, ids: (0, 0, 0)),
            scratch_shapes=[
                pltpu.VMEM((count * TOK, width), F32),
                pltpu.VMEM((planes, near, rows, width), BF16),
            ],
        ),
        out_shape=jax.ShapeDtypeStruct((count, TOK, width), BF16),
        cost_estimate=pl.CostEstimate(
            flops=2 * count * TOK * width * depth,
            bytes_accessed=2 * (count * TOK * (depth + width) + depth * width),
            transcendentals=0,
        ),
        name="upstream",
    )(ids, *pieces, *weights)


def proj_kernel(ids_ref, *refs):
    pieces, (ot_ref, a_ref, b_ref, lhs_ref) = refs[:-4], refs[-4:]
    count = len(pieces)
    near = a_ref.shape[0]
    split = a_ref.shape[2]

    @pl.when(pl.program_id(0) == 0)
    def _():
        for p in range(count):
            lhs_ref[:, p * TOK : (p + 1) * TOK] = ot_ref[ids_ref[p]]

    rows = jnp.concatenate([piece[...] for piece in pieces], 0)
    out = jnp.dot(lhs_ref[...], rows, preferred_element_type=F32).astype(BF16)
    for t in range(near):
        part = out[:, t * TOK : (t + 1) * TOK]
        a_ref[lax.rem(t + near - ids_ref[count + 1], near), 0] = part[:split]
        b_ref[0, t] = part[split:]


def proj_terms(ids, pieces, ot):
    count, width, _ = ot.shape
    far, near = GRID["dp"], GRID["fsdp"]
    split = width * 3 // 4
    depth = pieces[0].shape[1]

    return pl.pallas_call(
        proj_kernel,
        grid_spec=pltpu.PrefetchScalarGridSpec(
            num_scalar_prefetch=1,
            grid=(far,),
            in_specs=[pl.BlockSpec((TOK, near * TOK), lambda i, ids: (0, i))] * count
            + [pl.BlockSpec(ot.shape, lambda i, ids: (0, 0, 0))],
            out_specs=[
                pl.BlockSpec((near, 1, split, TOK), lambda i, ids: (0, lax.rem(i + far - ids[count], far), 0, 0)),
                pl.BlockSpec((1, near, width - split, TOK), lambda i, ids: (i, 0, 0, 0)),
            ],
            scratch_shapes=[pltpu.VMEM((width, count * TOK), BF16)],
        ),
        out_shape=[
            jax.ShapeDtypeStruct((near, far, split, TOK), BF16),
            jax.ShapeDtypeStruct((far, near, width - split, TOK), BF16),
        ],
        cost_estimate=pl.CostEstimate(
            flops=2 * count * TOK * width * depth,
            bytes_accessed=2 * (count * TOK * (depth + width) + depth * width),
            transcendentals=0,
        ),
        name="proj_terms",
    )(ids, *pieces, ot)


def shift(x, axis, by):
    n = GRID[axis]
    return lax.ppermute(x, axis, [(i, (i + by) % n) for i in range(n)])


def add(a, b):
    return (a.astype(F32) + b.astype(F32)).astype(BF16)


def after(value, done):
    return lax.optimization_barrier((value, done))[0]


def swap(x, axis):
    return lax.all_to_all(x, axis, split_axis=0, concat_axis=0, tiled=True)


def hop(x, chips, core):
    pairs = [(i * 2 + c, ((i + chips) % 4) * 2 + (c ^ core)) for i in range(4) for c in range(2)]
    return lax.ppermute(x, "seq", pairs)


def per_device(
    query_rows, forward_key_rows, forward_value_rows, out_cotangent, proj_weight, sent_lengths
):
    place = lax.axis_index("seq").astype(jnp.int32)
    chip, core = place // 2, place % 2
    chips = (chip + jnp.array([0, 3, 1, 2], jnp.int32)) % 4 * 2
    ids = jnp.concatenate(
        [
            chips + core,
            chips + 1 - core,
            jnp.stack([lax.axis_index("dp"), lax.axis_index("fsdp")]).astype(jnp.int32),
        ]
    )
    targets = (chip + jnp.array([0, 1, 3, 2], jnp.int32)) % 4 * 2
    targets = jnp.concatenate([targets + core, targets + 1 - core])
    far = GRID["dp"] // 2
    half = TOK // 2
    own = out_cotangent[0]
    left, right = hop(own, 1, 0), hop(own, -1, 0)
    weight = jnp.broadcast_to(proj_weight, (2 * far, *proj_weight.shape))
    weight = swap(weight, "dp")
    packed = pack(targets, query_rows, forward_key_rows, forward_value_rows)
    paths = [(chips, flip) for flip in range(2) for chips in (0, 1, -1, 2)]
    packed = [packed[0]] + [hop(x, *path) for x, path in zip(packed[1:], paths[1:])]
    partner = hop(own, 0, 1)
    below, above = shift(weight, "fsdp", 1), shift(weight, "fsdp", -1)
    lo, hi = limits(sent_lengths[0], len(packed))
    across = [hop(left[:half], 1, 0), hop(right[half:], -1, 0)]
    across = jnp.concatenate(across, 0)
    output = attend(ids, packed, lo, hi)
    pieces = [own, left, right, across, partner]
    pieces += [hop(piece, 0, 1) for piece in (left, right, across)]
    ends = [shift(below[:far], "fsdp", 1), shift(above[far:], "fsdp", -1)]
    first, second = proj_terms(ids, pieces, output)
    second = swap(second, "dp")
    up, down = shift(first[2, :far], "fsdp", 1), shift(first[2, far:], "fsdp", -1)
    arriving = upstream(ids, pieces, [weight, below, above, *ends])
    up, down = after((up, down), arriving)
    up = shift(jnp.concatenate([add(first[1, :far], up), first[1, far:]], 0), "fsdp", 1)
    down = shift(jnp.concatenate([first[3, :far], add(first[3, far:], down)], 0), "fsdp", -1)
    grads = attend_grad(ids, packed, arriving, lo, hi)
    grads_home = swap(grads, "seq")
    up, down, second = after((up, down, second), grads)
    first = (first[0].astype(F32) + up.astype(F32) + down.astype(F32)).astype(BF16)
    part = first.shape[1] // 2
    up, down = shift(first[4, :part], "dp", 1), shift(first[4, part:], "dp", -1)
    up = jnp.concatenate([add(first[3, :part], up), first[3, part:]], 0)
    down = jnp.concatenate([first[5, :part], add(first[5, part:], down)], 0)
    up, down = shift(up, "dp", 1), shift(down, "dp", -1)
    up, down = add(first[2], up), add(first[6], down)
    up, down = shift(up, "dp", 1), shift(down, "dp", -1)
    up, down = add(first[1], up), add(first[7], down)
    up, down = shift(up, "dp", 1), shift(down, "dp", -1)
    second = jnp.sum(second.astype(F32), axis=0).astype(BF16)
    second = swap(second, "fsdp")
    first = first[0].astype(F32) + up.astype(F32) + down.astype(F32)
    proj_grad = jnp.concatenate([first, jnp.sum(second.astype(F32), axis=0)], 0)
    query_grad, key_gradient, value_gradient = unpack(grads_home)
    return (query_grad, key_gradient, value_gradient, proj_grad.T.astype(BF16))


def solution(mesh):
    in_specs = (
        P(("dp", "fsdp"), "seq", None),
        P(("dp", "fsdp"), "seq", None),
        P(("dp", "fsdp"), "seq", None),
        P(("dp", "fsdp"), "seq", None),
        P(("dp", "fsdp"), "seq"),
        P(("dp", "fsdp"), None),
    )
    out_specs = (
        P(("dp", "fsdp"), "seq", None),
        P(("dp", "fsdp"), "seq", None),
        P(("dp", "fsdp"), "seq", None),
        P(("dp", "fsdp"), "seq"),
    )
    return jax.shard_map(
        per_device, mesh=mesh, in_specs=in_specs, out_specs=out_specs, check_vma=False
    )
```

```python
import math

import jax
import jax.numpy as jnp
from jax import lax
from jax.experimental import pallas as pl
from jax.experimental.pallas import tpu as pltpu
from jax.sharding import PartitionSpec as P

HEADS = 4
HEAD = 128
TOK = 128
KW = 448
FACTOR = 1.0 / math.sqrt(HEAD)
F32 = jnp.float32
BF16 = jnp.bfloat16
GROUP = 4
GRID = {"dp": 8, "fsdp": 4}


def window_start(i, blocks):
    return pl.multiple_of(jnp.clip(i * TOK - 256, 0, blocks * TOK - KW), 64)


def probs(i, start, q_ref, lo_ref, hi_ref, key, h0):
    q = jnp.concatenate(
        [q_ref[i, :, (h0 + j) * HEAD : (h0 + j + 1) * HEAD] for j in range(GROUP)], 0
    )
    s = lax.dot_general(key, q, (((1,), (1,)), ((), ())), preferred_element_type=F32)
    place = start + lax.broadcasted_iota(jnp.int32, (KW, GROUP * TOK), 0)
    lo = jnp.concatenate([lo_ref[i]] * GROUP, 1)
    hi = jnp.concatenate([hi_ref[i]] * GROUP, 1)
    p = jnp.where((place >= lo) & (place < hi), jnp.exp(s * FACTOR), 0.0)
    a = p * (1.0 / jnp.sum(p, axis=0, keepdims=True))
    return q, a


def assemble(ids_ref, pieces, q_ref, k_ref, v_ref):
    for p, piece in enumerate(pieces):
        b = ids_ref[p]
        rows = pl.ds(pl.multiple_of(b * TOK, TOK), TOK)
        q_ref[b] = piece[:, : HEADS * HEAD]
        k_ref[rows, :] = piece[:, HEADS * HEAD : (HEADS + 1) * HEAD]
        v_ref[rows, :] = piece[:, (HEADS + 1) * HEAD :]


def fwd_kernel(ids_ref, *refs):
    pieces, (lo_ref, hi_ref, o_ref, q_ref, k_ref, v_ref) = refs[:-6], refs[-6:]
    blocks = len(pieces)
    i = pl.program_id(0)

    @pl.when(i == 0)
    def _():
        assemble(ids_ref, pieces, q_ref, k_ref, v_ref)

    start = window_start(i, blocks)
    key = k_ref[pl.ds(start, KW), :]
    vt = v_ref[pl.ds(start, KW), :].T
    for h0 in range(0, HEADS, GROUP):
        _, a = probs(i, start, q_ref, lo_ref, hi_ref, key, h0)
        o = jnp.dot(vt, a.astype(BF16), preferred_element_type=F32).astype(BF16)
        for j in range(GROUP):
            o_ref[0, (h0 + j) * HEAD : (h0 + j + 1) * HEAD, :] = o[:, j * TOK : (j + 1) * TOK]


def bwd_kernel(ids_ref, *refs):
    blocks = (len(refs) - 9) // 2
    pieces, (u_ref, lo_ref, hi_ref) = refs[:blocks], refs[blocks : blocks + 3]
    homes, scratch = refs[blocks + 3 : -6], refs[-6:]
    o_ref, dk_ref, dv_ref, q_ref, k_ref, v_ref = scratch
    i = pl.program_id(0)

    @pl.when(i == 0)
    def _():
        assemble(ids_ref, pieces, q_ref, k_ref, v_ref)
        dk_ref[...] = jnp.zeros_like(dk_ref)
        dv_ref[...] = jnp.zeros_like(dv_ref)

    start = window_start(i, blocks)
    key = k_ref[pl.ds(start, KW), :]
    val = v_ref[pl.ds(start, KW), :]
    kt = key.T
    dk = None
    for h0 in range(0, HEADS, GROUP):
        q, a = probs(i, start, q_ref, lo_ref, hi_ref, key, h0)
        u = jnp.concatenate(
            [u_ref[i, :, (h0 + j) * HEAD : (h0 + j + 1) * HEAD] for j in range(GROUP)], 0
        )
        g = lax.dot_general(val, u, (((1,), (1,)), ((), ())), preferred_element_type=F32)
        delta = jnp.sum(a * g, axis=0, keepdims=True)
        ds = (a * (g - delta) * FACTOR).astype(BF16)
        dq = jnp.dot(kt, ds, preferred_element_type=F32)
        for j in range(GROUP):
            o_ref[i, :, (h0 + j) * HEAD : (h0 + j + 1) * HEAD] = dq[
                :, j * TOK : (j + 1) * TOK
            ].T.astype(BF16)
        dkh = jnp.dot(ds, q, preferred_element_type=F32)
        dvh = jnp.dot(a.astype(BF16), u, preferred_element_type=F32)
        dk, dv = (dkh, dvh) if dk is None else (dk + dkh, dv + dvh)
    dk_ref[pl.ds(start, KW), :] += dk
    dv_ref[pl.ds(start, KW), :] += dv

    @pl.when(i == blocks - 1)
    def _():
        for p, home in enumerate(homes):
            b = ids_ref[blocks + 2 + p]
            rows = pl.ds(pl.multiple_of(b * TOK, TOK), TOK)
            home[:, : HEADS * HEAD] = o_ref[b]
            home[:, HEADS * HEAD : (HEADS + 1) * HEAD] = dk_ref[rows, :].astype(BF16)
            home[:, (HEADS + 1) * HEAD :] = dv_ref[rows, :].astype(BF16)


def whole(shape):
    return pl.BlockSpec(shape, lambda i, ids: (0,) * len(shape))


def limits(sent_lengths, blocks):
    number = sent_lengths.shape[0]
    order = jnp.arange(number, dtype=jnp.int32)
    ends = jnp.sum(jnp.where(order[None, :] <= order[:, None], sent_lengths[None, :], 0), axis=1)
    places = jnp.arange(blocks * TOK, dtype=jnp.int32)
    sentence = jnp.sum((places[:, None] >= ends[None, :]).astype(jnp.int32), axis=1)
    lo = jnp.sum(
        jnp.where(order[None, :] + 3 < sentence[:, None], sent_lengths[None, :], 0), axis=1
    )
    hi = jnp.sum(jnp.where(order[None, :] <= sentence[:, None], sent_lengths[None, :], 0), axis=1)
    return lo.reshape(blocks, 1, TOK), hi.reshape(blocks, 1, TOK)


def head_scratch(blocks):
    keys = pltpu.VMEM((blocks * TOK, HEAD), BF16)
    return [pltpu.VMEM((blocks, TOK, HEADS * HEAD), BF16), keys, keys]


def attend(ids, pieces, lo, hi):
    blocks = len(pieces)
    pairs = blocks * TOK * KW * HEADS
    return pl.pallas_call(
        fwd_kernel,
        grid_spec=pltpu.PrefetchScalarGridSpec(
            num_scalar_prefetch=1,
            grid=(blocks,),
            in_specs=[whole(x.shape) for x in (*pieces, lo, hi)],
            out_specs=pl.BlockSpec((1, HEADS * HEAD, TOK), lambda i, ids: (i, 0, 0)),
            scratch_shapes=head_scratch(blocks),
        ),
        out_shape=jax.ShapeDtypeStruct((blocks, HEADS * HEAD, TOK), BF16),
        cost_estimate=pl.CostEstimate(
            flops=4 * pairs * HEAD,
            bytes_accessed=4 * blocks * pieces[0].size,
            transcendentals=pairs,
        ),
        name="attend",
    )(ids, *pieces, lo, hi)


def attend_grad(ids, pieces, u, lo, hi):
    blocks = len(pieces)
    pairs = blocks * TOK * KW * HEADS
    shape = pieces[0].shape
    return pl.pallas_call(
        bwd_kernel,
        grid_spec=pltpu.PrefetchScalarGridSpec(
            num_scalar_prefetch=1,
            grid=(blocks,),
            in_specs=[whole(x.shape) for x in (*pieces, u, lo, hi)],
            out_specs=[whole(shape)] * blocks,
            scratch_shapes=[pltpu.VMEM((blocks, TOK, HEADS * HEAD), BF16)]
            + [pltpu.VMEM((blocks * TOK, HEAD), F32)] * 2
            + head_scratch(blocks),
        ),
        out_shape=[jax.ShapeDtypeStruct(shape, BF16)] * blocks,
        cost_estimate=pl.CostEstimate(
            flops=10 * pairs * HEAD,
            bytes_accessed=6 * blocks * pieces[0].size,
            transcendentals=pairs,
        ),
        name="attend_grad",
    )(ids, *pieces, u, lo, hi)


def pack_kernel(ids_ref, q_ref, k_ref, v_ref, *o_refs):
    wide = HEADS * HEAD
    for p, o_ref in enumerate(o_refs):
        g = ids_ref[p]
        heads = pl.ds(pl.multiple_of(g * HEAD, HEAD), HEAD)
        o_ref[:, :wide] = q_ref[0, :, pl.ds(pl.multiple_of(g * wide, wide), wide)]
        o_ref[:, wide : wide + HEAD] = k_ref[0, :, heads]
        o_ref[:, wide + HEAD :] = v_ref[0, :, heads]


def pack(ids, q, k, v):
    groups = k.shape[2] // HEAD
    width = (HEADS + 2) * HEAD
    return pl.pallas_call(
        pack_kernel,
        grid_spec=pltpu.PrefetchScalarGridSpec(
            num_scalar_prefetch=1,
            grid=(1,),
            in_specs=[whole(x.shape) for x in (q, k, v)],
            out_specs=[whole((TOK, width))] * groups,
        ),
        out_shape=[jax.ShapeDtypeStruct((TOK, width), BF16)] * groups,
        cost_estimate=pl.CostEstimate(flops=0, bytes_accessed=6 * q.size, transcendentals=0),
        name="pack",
    )(ids, q, k, v)


def unpack_kernel(ids_ref, *refs):
    wide = HEADS * HEAD
    pieces, (q_ref, k_ref, v_ref) = refs[:-3], refs[-3:]
    for p, piece in enumerate(pieces):
        g = ids_ref[p]
        heads = pl.ds(pl.multiple_of(g * HEAD, HEAD), HEAD)
        q_ref[0, :, pl.ds(pl.multiple_of(g * wide, wide), wide)] = piece[:, :wide]
        k_ref[0, :, heads] = piece[:, wide : wide + HEAD]
        v_ref[0, :, heads] = piece[:, wide + HEAD :]


def unpack(ids, pieces):
    groups = len(pieces)
    shapes = [(1, TOK, groups * part) for part in (HEADS * HEAD, HEAD, HEAD)]
    return pl.pallas_call(
        unpack_kernel,
        grid_spec=pltpu.PrefetchScalarGridSpec(
            num_scalar_prefetch=1,
            grid=(1,),
            in_specs=[whole(x.shape) for x in pieces],
            out_specs=[whole(shape) for shape in shapes],
        ),
        out_shape=[jax.ShapeDtypeStruct(shape, BF16) for shape in shapes],
        cost_estimate=pl.CostEstimate(
            flops=0, bytes_accessed=4 * groups * pieces[0].size, transcendentals=0
        ),
        name="unpack",
    )(ids, *pieces)


def upstream_kernel(ids_ref, *refs):
    pieces, weights, (o_ref, acc_ref, w_ref) = refs[:-8], refs[-8:-3], refs[-3:]
    count = len(pieces)
    near = w_ref.shape[1]
    step = pl.program_id(0)
    last = pl.num_programs(0) - 1
    y = ids_ref[count + 1]
    mine, below, above, far_low, far_high = weights
    w_ref[:, y] = mine[...]
    w_ref[:, lax.rem(y + near - 1, near)] = below[...]
    w_ref[:, lax.rem(y + 1, near)] = above[...]

    @pl.when(step * 2 <= last)
    def _():
        w_ref[:, lax.rem(y + 2, near)] = far_low[...]

    @pl.when(step * 2 > last)
    def _():
        w_ref[:, lax.rem(y + 2, near)] = far_high[...]

    rows = jnp.concatenate([piece[...] for piece in pieces], 0)
    weight = w_ref[...].reshape(rows.shape[1], w_ref.shape[3])
    part = jnp.dot(rows, weight, preferred_element_type=F32)

    @pl.when(step == 0)
    def _():
        acc_ref[...] = part

    @pl.when(step > 0)
    def _():
        acc_ref[...] += part

    @pl.when(step == last)
    def _():
        for p in range(count):
            o_ref[ids_ref[p]] = acc_ref[p * TOK : (p + 1) * TOK, :].astype(BF16)


def upstream(ids, pieces, weights):
    far, rows, width = weights[0].shape
    near = GRID["fsdp"]
    depth = far * near * rows
    planes = 2
    steps = far // planes
    count = len(pieces)
    block = (planes, rows, width)
    return pl.pallas_call(
        upstream_kernel,
        grid_spec=pltpu.PrefetchScalarGridSpec(
            num_scalar_prefetch=1,
            grid=(steps,),
            in_specs=[pl.BlockSpec((TOK, depth // steps), lambda i, ids: (0, i))] * count
            + [pl.BlockSpec(block, lambda i, ids: (i, 0, 0))] * 3
            + [
                pl.BlockSpec(block, lambda i, ids: (jnp.minimum(i, steps // 2 - 1), 0, 0)),
                pl.BlockSpec(block, lambda i, ids: (jnp.maximum(i - steps // 2, 0), 0, 0)),
            ],
            out_specs=pl.BlockSpec((count, TOK, width), lambda i, ids: (0, 0, 0)),
            scratch_shapes=[
                pltpu.VMEM((count * TOK, width), F32),
                pltpu.VMEM((planes, near, rows, width), BF16),
            ],
        ),
        out_shape=jax.ShapeDtypeStruct((count, TOK, width), BF16),
        cost_estimate=pl.CostEstimate(
            flops=2 * count * TOK * width * depth,
            bytes_accessed=2 * (count * TOK * (depth + width) + depth * width),
            transcendentals=0,
        ),
        name="upstream",
    )(ids, *pieces, *weights)


def proj_kernel(ids_ref, *refs):
    pieces, refs = refs[:-8], refs[-8:]
    ot_ref, same_ref, next_ref, low_ref, high_ref, last_ref, lhs_ref, out_ref = refs
    count = len(pieces)
    near = GRID["fsdp"]
    step = pl.program_id(0)
    middle = pl.num_programs(0) // 2

    @pl.when(step == 0)
    def _():
        for p in range(count):
            lhs_ref[:, p * TOK : (p + 1) * TOK] = ot_ref[ids_ref[p]]

    rows = jnp.concatenate([piece[...] for piece in pieces], 0)
    out_ref[...] = jnp.dot(lhs_ref[...], rows, preferred_element_type=F32).astype(BF16)

    def part(offset):
        t = lax.rem(ids_ref[count + 1] + offset, near)
        return out_ref[:, pl.ds(pl.multiple_of(t * TOK, TOK), TOK)]

    same_ref[0] = part(0)
    next_ref[0] = part(1)
    last_ref[0] = part(3)

    @pl.when(step < middle)
    def _():
        low_ref[0] = part(2)

    @pl.when(step >= middle)
    def _():
        high_ref[0] = part(2)


def proj_terms(ids, pieces, ot):
    count, width, _ = ot.shape
    far, near = GRID["dp"], GRID["fsdp"]
    depth = pieces[0].shape[1]
    middle = far // 2
    block = (1, width, TOK)

    def plane(i, ids):
        return (i, 0, 0)

    full = jax.ShapeDtypeStruct((far, width, TOK), BF16)
    part = jax.ShapeDtypeStruct((middle, width, TOK), BF16)
    return pl.pallas_call(
        proj_kernel,
        grid_spec=pltpu.PrefetchScalarGridSpec(
            num_scalar_prefetch=1,
            grid=(far,),
            in_specs=[pl.BlockSpec((TOK, near * TOK), lambda i, ids: (0, i))] * count
            + [pl.BlockSpec(ot.shape, lambda i, ids: (0, 0, 0))],
            out_specs=[
                pl.BlockSpec(block, plane),
                pl.BlockSpec(block, plane),
                pl.BlockSpec(block, lambda i, ids: (jnp.minimum(i, middle - 1), 0, 0)),
                pl.BlockSpec(block, lambda i, ids: (jnp.maximum(i - middle, 0), 0, 0)),
                pl.BlockSpec(block, plane),
            ],
            scratch_shapes=[
                pltpu.VMEM((width, count * TOK), BF16),
                pltpu.VMEM((width, near * TOK), BF16),
            ],
        ),
        out_shape=[full, full, part, part, full],
        cost_estimate=pl.CostEstimate(
            flops=2 * count * TOK * width * depth,
            bytes_accessed=2 * (count * TOK * (depth + width) + depth * width),
            transcendentals=0,
        ),
        name="proj_terms",
    )(ids, *pieces, ot)


def join_kernel(low_ref, up_ref, high_ref, down_ref, low_out, high_out):
    low_out[...] = add(low_ref[...], up_ref[...])
    high_out[...] = add(high_ref[...], down_ref[...])


def join(low, up, high, down):
    planes, width, _ = up.shape
    block = (planes // 2, width, TOK)

    def front(i):
        return (i, 0, 0)

    def back(i):
        return (i + 2, 0, 0)

    return pl.pallas_call(
        join_kernel,
        grid=(2,),
        in_specs=[
            pl.BlockSpec(block, front),
            pl.BlockSpec(block, front),
            pl.BlockSpec(block, back),
            pl.BlockSpec(block, front),
        ],
        out_specs=[pl.BlockSpec(block, front), pl.BlockSpec(block, back)],
        out_shape=[jax.ShapeDtypeStruct(low.shape, BF16)] * 2,
        input_output_aliases={0: 0, 2: 1},
        cost_estimate=pl.CostEstimate(
            flops=2 * up.size, bytes_accessed=12 * up.size, transcendentals=0
        ),
        name="join",
    )(low, up, high, down)


def shift(x, axis, by):
    n = GRID[axis]
    return lax.ppermute(x, axis, [(i, (i + by) % n) for i in range(n)])


def add(a, b):
    return (a.astype(F32) + b.astype(F32)).astype(BF16)


def after(value, done):
    return lax.optimization_barrier((value, done))[0]


def swap(x, axis):
    return lax.all_to_all(x, axis, split_axis=0, concat_axis=0, tiled=True)


def hop(x, chips, core):
    pairs = [(i * 2 + c, ((i + chips) % 4) * 2 + (c ^ core)) for i in range(4) for c in range(2)]
    return lax.ppermute(x, "seq", pairs)


def per_device(
    query_rows, forward_key_rows, forward_value_rows, out_cotangent, proj_weight, sent_lengths
):
    place = lax.axis_index("seq").astype(jnp.int32)
    chip, core = place // 2, place % 2
    chips = (chip + jnp.array([0, 3, 1, 2], jnp.int32)) % 4 * 2
    ids = jnp.concatenate(
        [
            chips + core,
            chips + 1 - core,
            jnp.stack([lax.axis_index("dp"), lax.axis_index("fsdp")]).astype(jnp.int32),
        ]
    )
    targets = (chip + jnp.array([0, 1, 3, 2], jnp.int32)) % 4 * 2
    targets = jnp.concatenate([targets + core, targets + 1 - core])
    far = GRID["dp"] // 2
    half = TOK // 2
    own = out_cotangent[0]
    left, right = hop(own, 1, 0), hop(own, -1, 0)
    weight = jnp.broadcast_to(proj_weight, (2 * far, *proj_weight.shape))
    weight = swap(weight, "dp")
    packed = pack(targets, query_rows, forward_key_rows, forward_value_rows)
    paths = [(chips, flip) for flip in range(2) for chips in (0, 1, -1, 2)]
    packed = [packed[0]] + [hop(x, *path) for x, path in zip(packed[1:], paths[1:])]
    partner = hop(own, 0, 1)
    below, above = shift(weight, "fsdp", 1), shift(weight, "fsdp", -1)
    lo, hi = limits(sent_lengths[0], len(packed))
    across = [hop(left[:half], 1, 0), hop(right[half:], -1, 0)]
    across = jnp.concatenate(across, 0)
    output = attend(ids, packed, lo, hi)
    pieces = [own, left, right, across, partner]
    pieces += [hop(piece, 0, 1) for piece in (left, right, across)]
    same, following, low, high, before = proj_terms(ids, pieces, output)
    up, down = shift(low, "fsdp", 1), shift(high, "fsdp", -1)
    below, above = after((below, above), low)
    ends = [shift(below[:far], "fsdp", 1), shift(above[far:], "fsdp", -1)]
    following, before = join(following, up, before, down)
    up, down = shift(following, "fsdp", 1), shift(before, "fsdp", -1)
    arriving = upstream(ids, pieces, [weight, below, above, *ends])
    grads = attend_grad(jnp.concatenate([ids, targets]), packed, arriving, lo, hi)
    up, down = after((up, down), grads[0])
    first = (same.astype(F32) + up.astype(F32) + down.astype(F32)).astype(BF16)
    first = swap(first, "dp")
    grads = [grads[0]] + [hop(x, *path) for x, path in zip(grads[1:], paths[1:])]
    proj_grad = jnp.sum(first.astype(F32), axis=0).T.astype(BF16)
    query_grad, key_gradient, value_gradient = unpack(ids, grads)
    return (query_grad, key_gradient, value_gradient, proj_grad)


def solution(mesh):
    in_specs = (
        P(("dp", "fsdp"), "seq", None),
        P(("dp", "fsdp"), "seq", None),
        P(("dp", "fsdp"), "seq", None),
        P(("dp", "fsdp"), "seq", None),
        P(("dp", "fsdp"), "seq"),
        P(("dp", "fsdp"), None),
    )
    out_specs = (
        P(("dp", "fsdp"), "seq", None),
        P(("dp", "fsdp"), "seq", None),
        P(("dp", "fsdp"), "seq", None),
        P(("dp", "fsdp"), "seq"),
    )
    return jax.shard_map(
        per_device, mesh=mesh, in_specs=in_specs, out_specs=out_specs, check_vma=False
    )
```

```python
import math

import jax
import jax.numpy as jnp
from jax import lax
from jax.experimental import pallas as pl
from jax.experimental.pallas import tpu as pltpu
from jax.sharding import PartitionSpec as P

HEADS = 4
HEAD = 128
TOK = 128
KW = 448
FACTOR = 1.0 / math.sqrt(HEAD)
F32 = jnp.float32
BF16 = jnp.bfloat16
GROUP = 4
GRID = {"dp": 8, "fsdp": 4}


def window_start(i, blocks):
    return pl.multiple_of(jnp.clip(i * TOK - 256, 0, blocks * TOK - KW), 64)


def probs(i, start, q_ref, lo_ref, hi_ref, key, h0):
    q = jnp.concatenate(
        [q_ref[i, :, (h0 + j) * HEAD : (h0 + j + 1) * HEAD] for j in range(GROUP)], 0
    )
    s = lax.dot_general(key, q, (((1,), (1,)), ((), ())), preferred_element_type=F32)
    place = start + lax.broadcasted_iota(jnp.int32, (KW, GROUP * TOK), 0)
    lo = jnp.concatenate([lo_ref[i]] * GROUP, 1)
    hi = jnp.concatenate([hi_ref[i]] * GROUP, 1)
    p = jnp.where((place >= lo) & (place < hi), jnp.exp(s * FACTOR), 0.0)
    a = p * (1.0 / jnp.sum(p, axis=0, keepdims=True))
    return q, a


def assemble(ids_ref, pieces, q_ref, k_ref, v_ref):
    for p, piece in enumerate(pieces):
        b = ids_ref[p]
        rows = pl.ds(pl.multiple_of(b * TOK, TOK), TOK)
        q_ref[b] = piece[:, : HEADS * HEAD]
        k_ref[rows, :] = piece[:, HEADS * HEAD : (HEADS + 1) * HEAD]
        v_ref[rows, :] = piece[:, (HEADS + 1) * HEAD :]


def fwd_kernel(ids_ref, *refs):
    pieces, (lo_ref, hi_ref, o_ref, q_ref, k_ref, v_ref) = refs[:-6], refs[-6:]
    blocks = len(pieces)
    i = pl.program_id(0)

    @pl.when(i == 0)
    def _():
        assemble(ids_ref, pieces, q_ref, k_ref, v_ref)

    start = window_start(i, blocks)
    key = k_ref[pl.ds(start, KW), :]
    vt = v_ref[pl.ds(start, KW), :].T
    for h0 in range(0, HEADS, GROUP):
        _, a = probs(i, start, q_ref, lo_ref, hi_ref, key, h0)
        o = jnp.dot(vt, a.astype(BF16), preferred_element_type=F32).astype(BF16)
        for j in range(GROUP):
            o_ref[0, (h0 + j) * HEAD : (h0 + j + 1) * HEAD, :] = o[:, j * TOK : (j + 1) * TOK]


def bwd_kernel(ids_ref, *refs):
    blocks = (len(refs) - 9) // 2
    pieces, (u_ref, lo_ref, hi_ref) = refs[:blocks], refs[blocks : blocks + 3]
    homes, scratch = refs[blocks + 3 : -6], refs[-6:]
    o_ref, dk_ref, dv_ref, q_ref, k_ref, v_ref = scratch
    i = pl.program_id(0)

    @pl.when(i == 0)
    def _():
        assemble(ids_ref, pieces, q_ref, k_ref, v_ref)
        dk_ref[...] = jnp.zeros_like(dk_ref)
        dv_ref[...] = jnp.zeros_like(dv_ref)

    start = window_start(i, blocks)
    key = k_ref[pl.ds(start, KW), :]
    val = v_ref[pl.ds(start, KW), :]
    kt = key.T
    dk = None
    for h0 in range(0, HEADS, GROUP):
        q, a = probs(i, start, q_ref, lo_ref, hi_ref, key, h0)
        u = jnp.concatenate(
            [u_ref[i, :, (h0 + j) * HEAD : (h0 + j + 1) * HEAD] for j in range(GROUP)], 0
        )
        g = lax.dot_general(val, u, (((1,), (1,)), ((), ())), preferred_element_type=F32)
        delta = jnp.sum(a * g, axis=0, keepdims=True)
        ds = (a * (g - delta) * FACTOR).astype(BF16)
        dq = jnp.dot(kt, ds, preferred_element_type=F32)
        for j in range(GROUP):
            o_ref[i, :, (h0 + j) * HEAD : (h0 + j + 1) * HEAD] = dq[
                :, j * TOK : (j + 1) * TOK
            ].T.astype(BF16)
        dkh = jnp.dot(ds, q, preferred_element_type=F32)
        dvh = jnp.dot(a.astype(BF16), u, preferred_element_type=F32)
        dk, dv = (dkh, dvh) if dk is None else (dk + dkh, dv + dvh)
    dk_ref[pl.ds(start, KW), :] += dk
    dv_ref[pl.ds(start, KW), :] += dv

    @pl.when(i == blocks - 1)
    def _():
        for p, home in enumerate(homes):
            b = ids_ref[blocks + 2 + p]
            rows = pl.ds(pl.multiple_of(b * TOK, TOK), TOK)
            home[:, : HEADS * HEAD] = o_ref[b]
            home[:, HEADS * HEAD : (HEADS + 1) * HEAD] = dk_ref[rows, :].astype(BF16)
            home[:, (HEADS + 1) * HEAD :] = dv_ref[rows, :].astype(BF16)


def whole(shape):
    return pl.BlockSpec(shape, lambda i, ids: (0,) * len(shape))


def limits(sent_lengths, blocks):
    number = sent_lengths.shape[0]
    order = jnp.arange(number, dtype=jnp.int32)
    ends = jnp.sum(jnp.where(order[None, :] <= order[:, None], sent_lengths[None, :], 0), axis=1)
    places = jnp.arange(blocks * TOK, dtype=jnp.int32)
    sentence = jnp.sum((places[:, None] >= ends[None, :]).astype(jnp.int32), axis=1)
    lo = jnp.sum(
        jnp.where(order[None, :] + 3 < sentence[:, None], sent_lengths[None, :], 0), axis=1
    )
    hi = jnp.sum(jnp.where(order[None, :] <= sentence[:, None], sent_lengths[None, :], 0), axis=1)
    return lo.reshape(blocks, 1, TOK), hi.reshape(blocks, 1, TOK)


def head_scratch(blocks):
    keys = pltpu.VMEM((blocks * TOK, HEAD), BF16)
    return [pltpu.VMEM((blocks, TOK, HEADS * HEAD), BF16), keys, keys]


def attend(ids, pieces, lo, hi):
    blocks = len(pieces)
    pairs = blocks * TOK * KW * HEADS
    return pl.pallas_call(
        fwd_kernel,
        grid_spec=pltpu.PrefetchScalarGridSpec(
            num_scalar_prefetch=1,
            grid=(blocks,),
            in_specs=[whole(x.shape) for x in (*pieces, lo, hi)],
            out_specs=pl.BlockSpec((1, HEADS * HEAD, TOK), lambda i, ids: (i, 0, 0)),
            scratch_shapes=head_scratch(blocks),
        ),
        out_shape=jax.ShapeDtypeStruct((blocks, HEADS * HEAD, TOK), BF16),
        cost_estimate=pl.CostEstimate(
            flops=4 * pairs * HEAD,
            bytes_accessed=4 * blocks * pieces[0].size,
            transcendentals=pairs,
        ),
        name="attend",
    )(ids, *pieces, lo, hi)


def attend_grad(ids, pieces, u, lo, hi):
    blocks = len(pieces)
    pairs = blocks * TOK * KW * HEADS
    shape = pieces[0].shape
    return pl.pallas_call(
        bwd_kernel,
        grid_spec=pltpu.PrefetchScalarGridSpec(
            num_scalar_prefetch=1,
            grid=(blocks,),
            in_specs=[whole(x.shape) for x in (*pieces, u, lo, hi)],
            out_specs=[whole(shape)] * blocks,
            scratch_shapes=[pltpu.VMEM((blocks, TOK, HEADS * HEAD), BF16)]
            + [pltpu.VMEM((blocks * TOK, HEAD), F32)] * 2
            + head_scratch(blocks),
        ),
        out_shape=[jax.ShapeDtypeStruct(shape, BF16)] * blocks,
        cost_estimate=pl.CostEstimate(
            flops=10 * pairs * HEAD,
            bytes_accessed=6 * blocks * pieces[0].size,
            transcendentals=pairs,
        ),
        name="attend_grad",
    )(ids, *pieces, u, lo, hi)


def pack_kernel(ids_ref, q_ref, k_ref, v_ref, *o_refs):
    wide = HEADS * HEAD
    for p, o_ref in enumerate(o_refs):
        g = ids_ref[p]
        heads = pl.ds(pl.multiple_of(g * HEAD, HEAD), HEAD)
        o_ref[:, :wide] = q_ref[0, :, pl.ds(pl.multiple_of(g * wide, wide), wide)]
        o_ref[:, wide : wide + HEAD] = k_ref[0, :, heads]
        o_ref[:, wide + HEAD :] = v_ref[0, :, heads]


def pack(ids, q, k, v):
    groups = k.shape[2] // HEAD
    width = (HEADS + 2) * HEAD
    return pl.pallas_call(
        pack_kernel,
        grid_spec=pltpu.PrefetchScalarGridSpec(
            num_scalar_prefetch=1,
            grid=(1,),
            in_specs=[whole(x.shape) for x in (q, k, v)],
            out_specs=[whole((TOK, width))] * groups,
        ),
        out_shape=[jax.ShapeDtypeStruct((TOK, width), BF16)] * groups,
        cost_estimate=pl.CostEstimate(flops=0, bytes_accessed=6 * q.size, transcendentals=0),
        name="pack",
    )(ids, q, k, v)


def unpack_kernel(ids_ref, *refs):
    wide = HEADS * HEAD
    pieces, (q_ref, k_ref, v_ref) = refs[:-3], refs[-3:]
    for p, piece in enumerate(pieces):
        g = ids_ref[p]
        heads = pl.ds(pl.multiple_of(g * HEAD, HEAD), HEAD)
        q_ref[0, :, pl.ds(pl.multiple_of(g * wide, wide), wide)] = piece[:, :wide]
        k_ref[0, :, heads] = piece[:, wide : wide + HEAD]
        v_ref[0, :, heads] = piece[:, wide + HEAD :]


def unpack(ids, pieces):
    groups = len(pieces)
    shapes = [(1, TOK, groups * part) for part in (HEADS * HEAD, HEAD, HEAD)]
    return pl.pallas_call(
        unpack_kernel,
        grid_spec=pltpu.PrefetchScalarGridSpec(
            num_scalar_prefetch=1,
            grid=(1,),
            in_specs=[whole(x.shape) for x in pieces],
            out_specs=[whole(shape) for shape in shapes],
        ),
        out_shape=[jax.ShapeDtypeStruct(shape, BF16) for shape in shapes],
        cost_estimate=pl.CostEstimate(
            flops=0, bytes_accessed=4 * groups * pieces[0].size, transcendentals=0
        ),
        name="unpack",
    )(ids, *pieces)


def upstream_kernel(ids_ref, *refs):
    weights, (o_ref, acc_ref, w_ref) = refs[-11:-3], refs[-3:]
    pieces = refs[:-11]
    count = len(pieces)
    near = w_ref.shape[1]
    step = pl.program_id(0)
    last = pl.num_programs(0) - 1
    for offset in range(near):
        t = lax.rem(ids_ref[count + 1] + offset, near)
        left, right = weights[2 * offset], weights[2 * offset + 1]
        cut = left.shape[2]
        w_ref[:, t, :, :cut] = left[...]
        w_ref[:, t, :, cut:] = right[...]

    rows = jnp.concatenate([piece[...] for piece in pieces], 0)
    weight = w_ref[...].reshape(rows.shape[1], w_ref.shape[3])
    part = jnp.dot(rows, weight, preferred_element_type=F32)

    @pl.when(step == 0)
    def _():
        acc_ref[...] = part

    @pl.when(step > 0)
    def _():
        acc_ref[...] += part

    @pl.when(step == last)
    def _():
        for p in range(count):
            o_ref[ids_ref[p]] = acc_ref[p * TOK : (p + 1) * TOK, :].astype(BF16)


def upstream(ids, pieces, weights):
    far, rows, cut = weights[0].shape
    width = 2 * cut
    near = GRID["fsdp"]
    depth = far * near * rows
    planes = 2
    steps = far // planes
    count = len(pieces)
    return pl.pallas_call(
        upstream_kernel,
        grid_spec=pltpu.PrefetchScalarGridSpec(
            num_scalar_prefetch=1,
            grid=(steps,),
            in_specs=[pl.BlockSpec((TOK, depth // steps), lambda i, ids: (0, i))] * count
            + [pl.BlockSpec((planes, rows, cut), lambda i, ids: (i, 0, 0))] * (2 * near),
            out_specs=pl.BlockSpec((count, TOK, width), lambda i, ids: (0, 0, 0)),
            scratch_shapes=[
                pltpu.VMEM((count * TOK, width), F32),
                pltpu.VMEM((planes, near, rows, width), BF16),
            ],
        ),
        out_shape=jax.ShapeDtypeStruct((count, TOK, width), BF16),
        cost_estimate=pl.CostEstimate(
            flops=2 * count * TOK * width * depth,
            bytes_accessed=2 * (count * TOK * (depth + width) + depth * width),
            transcendentals=0,
        ),
        name="upstream",
    )(ids, *pieces, *weights)


def proj_kernel(ids_ref, *refs):
    pieces, refs = refs[:-8], refs[-8:]
    ot_ref, same_ref, next_ref, low_ref, high_ref, last_ref, lhs_ref, out_ref = refs
    count = len(pieces)
    near = GRID["fsdp"]
    step = pl.program_id(0)
    middle = pl.num_programs(0) // 2

    @pl.when(step == 0)
    def _():
        for p in range(count):
            lhs_ref[:, p * TOK : (p + 1) * TOK] = ot_ref[ids_ref[p]]

    rows = jnp.concatenate([piece[...] for piece in pieces], 0)
    out_ref[...] = jnp.dot(lhs_ref[...], rows, preferred_element_type=F32).astype(BF16)

    def part(offset):
        t = lax.rem(ids_ref[count + 1] + offset, near)
        return out_ref[:, pl.ds(pl.multiple_of(t * TOK, TOK), TOK)]

    same_ref[0] = part(0)
    next_ref[0] = part(1)
    last_ref[0] = part(3)

    @pl.when(step < middle)
    def _():
        low_ref[0] = part(2)

    @pl.when(step >= middle)
    def _():
        high_ref[0] = part(2)


def proj_terms(ids, pieces, ot):
    count, width, _ = ot.shape
    far, near = GRID["dp"], GRID["fsdp"]
    depth = pieces[0].shape[1]
    middle = far // 2
    block = (1, width, TOK)

    def plane(i, ids):
        return (i, 0, 0)

    full = jax.ShapeDtypeStruct((far, width, TOK), BF16)
    part = jax.ShapeDtypeStruct((middle, width, TOK), BF16)
    return pl.pallas_call(
        proj_kernel,
        grid_spec=pltpu.PrefetchScalarGridSpec(
            num_scalar_prefetch=1,
            grid=(far,),
            in_specs=[pl.BlockSpec((TOK, near * TOK), lambda i, ids: (0, i))] * count
            + [pl.BlockSpec(ot.shape, lambda i, ids: (0, 0, 0))],
            out_specs=[
                pl.BlockSpec(block, plane),
                pl.BlockSpec(block, plane),
                pl.BlockSpec(block, lambda i, ids: (jnp.minimum(i, middle - 1), 0, 0)),
                pl.BlockSpec(block, lambda i, ids: (jnp.maximum(i - middle, 0), 0, 0)),
                pl.BlockSpec(block, plane),
            ],
            scratch_shapes=[
                pltpu.VMEM((width, count * TOK), BF16),
                pltpu.VMEM((width, near * TOK), BF16),
            ],
        ),
        out_shape=[full, full, part, part, full],
        cost_estimate=pl.CostEstimate(
            flops=2 * count * TOK * width * depth,
            bytes_accessed=2 * (count * TOK * (depth + width) + depth * width),
            transcendentals=0,
        ),
        name="proj_terms",
    )(ids, *pieces, ot)


def join_kernel(low_ref, up_ref, high_ref, down_ref, low_out, high_out):
    low_out[...] = add(low_ref[...], up_ref[...])
    high_out[...] = add(high_ref[...], down_ref[...])


def join(low, up, high, down):
    planes, width, _ = up.shape
    block = (planes // 2, width, TOK)

    def front(i):
        return (i, 0, 0)

    def back(i):
        return (i + 2, 0, 0)

    return pl.pallas_call(
        join_kernel,
        grid=(2,),
        in_specs=[
            pl.BlockSpec(block, front),
            pl.BlockSpec(block, front),
            pl.BlockSpec(block, back),
            pl.BlockSpec(block, front),
        ],
        out_specs=[pl.BlockSpec(block, front), pl.BlockSpec(block, back)],
        out_shape=[jax.ShapeDtypeStruct(low.shape, BF16)] * 2,
        input_output_aliases={0: 0, 2: 1},
        cost_estimate=pl.CostEstimate(
            flops=2 * up.size, bytes_accessed=12 * up.size, transcendentals=0
        ),
        name="join",
    )(low, up, high, down)


def shift(x, axis, by):
    n = GRID[axis]
    return lax.ppermute(x, axis, [(i, (i + by) % n) for i in range(n)])


def add(a, b):
    return (a.astype(F32) + b.astype(F32)).astype(BF16)


def after(value, done):
    return lax.optimization_barrier((value, done))[0]


def swap(x, axis):
    return lax.all_to_all(x, axis, split_axis=0, concat_axis=0, tiled=True)


def hop(x, chips, core):
    pairs = [(i * 2 + c, ((i + chips) % 4) * 2 + (c ^ core)) for i in range(4) for c in range(2)]
    return lax.ppermute(x, "seq", pairs)


def per_device(
    query_rows, forward_key_rows, forward_value_rows, out_cotangent, proj_weight, sent_lengths
):
    place = lax.axis_index("seq").astype(jnp.int32)
    chip, core = place // 2, place % 2
    chips = (chip + jnp.array([0, 3, 1, 2], jnp.int32)) % 4 * 2
    ids = jnp.concatenate(
        [
            chips + core,
            chips + 1 - core,
            jnp.stack([lax.axis_index("dp"), lax.axis_index("fsdp")]).astype(jnp.int32),
        ]
    )
    targets = (chip + jnp.array([0, 1, 3, 2], jnp.int32)) % 4 * 2
    targets = jnp.concatenate([targets + core, targets + 1 - core])
    far = GRID["dp"] // 2
    half = TOK // 2
    own = out_cotangent[0]
    left, right = hop(own, 1, 0), hop(own, -1, 0)
    cut = proj_weight.shape[1] // 2
    left_half, right_half = (
        jnp.broadcast_to(x, (2 * far, *x.shape)) for x in jnp.split(proj_weight, [cut], axis=1)
    )
    left_half = swap(left_half, "dp")
    packed = pack(targets, query_rows, forward_key_rows, forward_value_rows)
    paths = [(chips, flip) for flip in range(2) for chips in (0, 1, -1, 2)]
    packed = [packed[0]] + [hop(x, *path) for x, path in zip(packed[1:], paths[1:])]
    partner = hop(own, 0, 1)
    right_half = swap(right_half, "dp")
    weights_left = [left_half] + [shift(left_half, "fsdp", -by) for by in (1, 2, 3)]
    weights_right = [right_half] + [shift(right_half, "fsdp", -by) for by in (1, 2, 3)]
    weights = [x for pair in zip(weights_left, weights_right) for x in pair]
    lo, hi = limits(sent_lengths[0], len(packed))
    across = [hop(left[:half], 1, 0), hop(right[half:], -1, 0)]
    across = jnp.concatenate(across, 0)
    output = attend(ids, packed, lo, hi)
    pieces = [own, left, right, across, partner]
    pieces += [hop(piece, 0, 1) for piece in (left, right, across)]
    same, following, low, high, before = proj_terms(ids, pieces, output)
    up, down = shift(low, "fsdp", 1), shift(high, "fsdp", -1)
    following, before = join(following, up, before, down)
    up, down = shift(following, "fsdp", 1), shift(before, "fsdp", -1)
    arriving = upstream(ids, pieces, weights)
    grads = attend_grad(jnp.concatenate([ids, targets]), packed, arriving, lo, hi)
    up, down = after((up, down), grads[0])
    first = (same.astype(F32) + up.astype(F32) + down.astype(F32)).astype(BF16)
    first = swap(first, "dp")
    grads = [grads[0]] + [hop(x, *path) for x, path in zip(grads[1:], paths[1:])]
    proj_grad = jnp.sum(first.astype(F32), axis=0).T.astype(BF16)
    query_grad, key_gradient, value_gradient = unpack(ids, grads)
    return (query_grad, key_gradient, value_gradient, proj_grad)


def solution(mesh):
    in_specs = (
        P(("dp", "fsdp"), "seq", None),
        P(("dp", "fsdp"), "seq", None),
        P(("dp", "fsdp"), "seq", None),
        P(("dp", "fsdp"), "seq", None),
        P(("dp", "fsdp"), "seq"),
        P(("dp", "fsdp"), None),
    )
    out_specs = (
        P(("dp", "fsdp"), "seq", None),
        P(("dp", "fsdp"), "seq", None),
        P(("dp", "fsdp"), "seq", None),
        P(("dp", "fsdp"), "seq"),
    )
    return jax.shard_map(
        per_device, mesh=mesh, in_specs=in_specs, out_specs=out_specs, check_vma=False
    )
```

```python
import math

import jax
import jax.numpy as jnp
from jax import lax
from jax.experimental import pallas as pl
from jax.experimental.pallas import tpu as pltpu
from jax.sharding import PartitionSpec as P

HEADS = 4
HEAD = 128
TOK = 128
KW = 448
FACTOR = 1.0 / math.sqrt(HEAD)
F32 = jnp.float32
BF16 = jnp.bfloat16
GROUP = 4
GRID = {"dp": 8, "fsdp": 4}


def window_start(i, blocks):
    return pl.multiple_of(jnp.clip(i * TOK - 256, 0, blocks * TOK - KW), 64)


def probs(i, start, q_ref, lo_ref, hi_ref, key, h0):
    q = jnp.concatenate(
        [q_ref[i, :, (h0 + j) * HEAD : (h0 + j + 1) * HEAD] for j in range(GROUP)], 0
    )
    s = lax.dot_general(key, q, (((1,), (1,)), ((), ())), preferred_element_type=F32)
    place = start + lax.broadcasted_iota(jnp.int32, (KW, GROUP * TOK), 0)
    lo = jnp.concatenate([lo_ref[i]] * GROUP, 1)
    hi = jnp.concatenate([hi_ref[i]] * GROUP, 1)
    p = jnp.where((place >= lo) & (place < hi), jnp.exp(s * FACTOR), 0.0)
    a = p * (1.0 / jnp.sum(p, axis=0, keepdims=True))
    return q, a


def assemble(ids_ref, pieces, q_ref, k_ref, v_ref):
    for p, piece in enumerate(pieces):
        b = ids_ref[p]
        rows = pl.ds(pl.multiple_of(b * TOK, TOK), TOK)
        q_ref[b] = piece[:, : HEADS * HEAD]
        k_ref[rows, :] = piece[:, HEADS * HEAD : (HEADS + 1) * HEAD]
        v_ref[rows, :] = piece[:, (HEADS + 1) * HEAD :]


def fwd_kernel(ids_ref, *refs):
    pieces, (lo_ref, hi_ref, o_ref, q_ref, k_ref, v_ref) = refs[:-6], refs[-6:]
    blocks = len(pieces)
    i = pl.program_id(0)

    @pl.when(i == 0)
    def _():
        assemble(ids_ref, pieces, q_ref, k_ref, v_ref)

    start = window_start(i, blocks)
    key = k_ref[pl.ds(start, KW), :]
    vt = v_ref[pl.ds(start, KW), :].T
    for h0 in range(0, HEADS, GROUP):
        _, a = probs(i, start, q_ref, lo_ref, hi_ref, key, h0)
        o = jnp.dot(vt, a.astype(BF16), preferred_element_type=F32).astype(BF16)
        for j in range(GROUP):
            o_ref[0, (h0 + j) * HEAD : (h0 + j + 1) * HEAD, :] = o[:, j * TOK : (j + 1) * TOK]


def bwd_kernel(ids_ref, *refs):
    blocks = (len(refs) - 9) // 2
    pieces, (u_ref, lo_ref, hi_ref) = refs[:blocks], refs[blocks : blocks + 3]
    homes, scratch = refs[blocks + 3 : -6], refs[-6:]
    o_ref, dk_ref, dv_ref, q_ref, k_ref, v_ref = scratch
    i = pl.program_id(0)

    @pl.when(i == 0)
    def _():
        assemble(ids_ref, pieces, q_ref, k_ref, v_ref)
        dk_ref[...] = jnp.zeros_like(dk_ref)
        dv_ref[...] = jnp.zeros_like(dv_ref)

    start = window_start(i, blocks)
    key = k_ref[pl.ds(start, KW), :]
    val = v_ref[pl.ds(start, KW), :]
    kt = key.T
    dk = None
    for h0 in range(0, HEADS, GROUP):
        q, a = probs(i, start, q_ref, lo_ref, hi_ref, key, h0)
        u = jnp.concatenate(
            [u_ref[i, :, (h0 + j) * HEAD : (h0 + j + 1) * HEAD] for j in range(GROUP)], 0
        )
        g = lax.dot_general(val, u, (((1,), (1,)), ((), ())), preferred_element_type=F32)
        delta = jnp.sum(a * g, axis=0, keepdims=True)
        ds = (a * (g - delta) * FACTOR).astype(BF16)
        dq = jnp.dot(kt, ds, preferred_element_type=F32)
        for j in range(GROUP):
            o_ref[i, :, (h0 + j) * HEAD : (h0 + j + 1) * HEAD] = dq[
                :, j * TOK : (j + 1) * TOK
            ].T.astype(BF16)
        dkh = jnp.dot(ds, q, preferred_element_type=F32)
        dvh = jnp.dot(a.astype(BF16), u, preferred_element_type=F32)
        dk, dv = (dkh, dvh) if dk is None else (dk + dkh, dv + dvh)
    dk_ref[pl.ds(start, KW), :] += dk
    dv_ref[pl.ds(start, KW), :] += dv

    @pl.when(i == blocks - 1)
    def _():
        for p, home in enumerate(homes):
            b = ids_ref[blocks + 2 + p]
            rows = pl.ds(pl.multiple_of(b * TOK, TOK), TOK)
            home[:, : HEADS * HEAD] = o_ref[b]
            home[:, HEADS * HEAD : (HEADS + 1) * HEAD] = dk_ref[rows, :].astype(BF16)
            home[:, (HEADS + 1) * HEAD :] = dv_ref[rows, :].astype(BF16)


def whole(shape):
    return pl.BlockSpec(shape, lambda i, ids: (0,) * len(shape))


def limits(sent_lengths, blocks):
    number = sent_lengths.shape[0]
    order = jnp.arange(number, dtype=jnp.int32)
    ends = jnp.sum(jnp.where(order[None, :] <= order[:, None], sent_lengths[None, :], 0), axis=1)
    places = jnp.arange(blocks * TOK, dtype=jnp.int32)
    sentence = jnp.sum((places[:, None] >= ends[None, :]).astype(jnp.int32), axis=1)
    lo = jnp.sum(
        jnp.where(order[None, :] + 3 < sentence[:, None], sent_lengths[None, :], 0), axis=1
    )
    hi = jnp.sum(jnp.where(order[None, :] <= sentence[:, None], sent_lengths[None, :], 0), axis=1)
    return lo.reshape(blocks, 1, TOK), hi.reshape(blocks, 1, TOK)


def head_scratch(blocks):
    keys = pltpu.VMEM((blocks * TOK, HEAD), BF16)
    return [pltpu.VMEM((blocks, TOK, HEADS * HEAD), BF16), keys, keys]


def attend(ids, pieces, lo, hi):
    blocks = len(pieces)
    pairs = blocks * TOK * KW * HEADS
    return pl.pallas_call(
        fwd_kernel,
        grid_spec=pltpu.PrefetchScalarGridSpec(
            num_scalar_prefetch=1,
            grid=(blocks,),
            in_specs=[whole(x.shape) for x in (*pieces, lo, hi)],
            out_specs=pl.BlockSpec((1, HEADS * HEAD, TOK), lambda i, ids: (i, 0, 0)),
            scratch_shapes=head_scratch(blocks),
        ),
        out_shape=jax.ShapeDtypeStruct((blocks, HEADS * HEAD, TOK), BF16),
        cost_estimate=pl.CostEstimate(
            flops=4 * pairs * HEAD,
            bytes_accessed=4 * blocks * pieces[0].size,
            transcendentals=pairs,
        ),
        name="attend",
    )(ids, *pieces, lo, hi)


def attend_grad(ids, pieces, u, lo, hi):
    blocks = len(pieces)
    pairs = blocks * TOK * KW * HEADS
    shape = pieces[0].shape
    return pl.pallas_call(
        bwd_kernel,
        grid_spec=pltpu.PrefetchScalarGridSpec(
            num_scalar_prefetch=1,
            grid=(blocks,),
            in_specs=[whole(x.shape) for x in (*pieces, u, lo, hi)],
            out_specs=[whole(shape)] * blocks,
            scratch_shapes=[pltpu.VMEM((blocks, TOK, HEADS * HEAD), BF16)]
            + [pltpu.VMEM((blocks * TOK, HEAD), F32)] * 2
            + head_scratch(blocks),
        ),
        out_shape=[jax.ShapeDtypeStruct(shape, BF16)] * blocks,
        cost_estimate=pl.CostEstimate(
            flops=10 * pairs * HEAD,
            bytes_accessed=6 * blocks * pieces[0].size,
            transcendentals=pairs,
        ),
        name="attend_grad",
    )(ids, *pieces, u, lo, hi)


def pack_kernel(ids_ref, q_ref, k_ref, v_ref, *o_refs):
    wide = HEADS * HEAD
    for p, o_ref in enumerate(o_refs):
        g = ids_ref[p]
        heads = pl.ds(pl.multiple_of(g * HEAD, HEAD), HEAD)
        o_ref[:, :wide] = q_ref[0, :, pl.ds(pl.multiple_of(g * wide, wide), wide)]
        o_ref[:, wide : wide + HEAD] = k_ref[0, :, heads]
        o_ref[:, wide + HEAD :] = v_ref[0, :, heads]


def pack(ids, q, k, v):
    groups = k.shape[2] // HEAD
    width = (HEADS + 2) * HEAD
    return pl.pallas_call(
        pack_kernel,
        grid_spec=pltpu.PrefetchScalarGridSpec(
            num_scalar_prefetch=1,
            grid=(1,),
            in_specs=[whole(x.shape) for x in (q, k, v)],
            out_specs=[whole((TOK, width))] * groups,
        ),
        out_shape=[jax.ShapeDtypeStruct((TOK, width), BF16)] * groups,
        cost_estimate=pl.CostEstimate(flops=0, bytes_accessed=6 * q.size, transcendentals=0),
        name="pack",
    )(ids, q, k, v)


def unpack_kernel(ids_ref, *refs):
    wide = HEADS * HEAD
    pieces, (q_ref, k_ref, v_ref) = refs[:-3], refs[-3:]
    for p, piece in enumerate(pieces):
        g = ids_ref[p]
        heads = pl.ds(pl.multiple_of(g * HEAD, HEAD), HEAD)
        q_ref[0, :, pl.ds(pl.multiple_of(g * wide, wide), wide)] = piece[:, :wide]
        k_ref[0, :, heads] = piece[:, wide : wide + HEAD]
        v_ref[0, :, heads] = piece[:, wide + HEAD :]


def unpack(ids, pieces):
    groups = len(pieces)
    shapes = [(1, TOK, groups * part) for part in (HEADS * HEAD, HEAD, HEAD)]
    return pl.pallas_call(
        unpack_kernel,
        grid_spec=pltpu.PrefetchScalarGridSpec(
            num_scalar_prefetch=1,
            grid=(1,),
            in_specs=[whole(x.shape) for x in pieces],
            out_specs=[whole(shape) for shape in shapes],
        ),
        out_shape=[jax.ShapeDtypeStruct(shape, BF16) for shape in shapes],
        cost_estimate=pl.CostEstimate(
            flops=0, bytes_accessed=4 * groups * pieces[0].size, transcendentals=0
        ),
        name="unpack",
    )(ids, *pieces)


def upstream_kernel(ids_ref, *refs):
    pieces, weights, (o_ref, acc_ref, w_ref) = refs[:-8], refs[-8:-3], refs[-3:]
    count = len(pieces)
    near = w_ref.shape[1]
    step = pl.program_id(0)
    last = pl.num_programs(0) - 1
    y = ids_ref[count + 1]
    mine, below, above, far_low, far_high = weights
    w_ref[:, y] = mine[...]
    w_ref[:, lax.rem(y + near - 1, near)] = below[...]
    w_ref[:, lax.rem(y + 1, near)] = above[...]

    @pl.when(step * 2 <= last)
    def _():
        w_ref[:, lax.rem(y + 2, near)] = far_low[...]

    @pl.when(step * 2 > last)
    def _():
        w_ref[:, lax.rem(y + 2, near)] = far_high[...]

    rows = jnp.concatenate([piece[...] for piece in pieces], 0)
    weight = w_ref[...].reshape(rows.shape[1], w_ref.shape[3])
    part = jnp.dot(rows, weight, preferred_element_type=F32)

    @pl.when(step == 0)
    def _():
        acc_ref[...] = part

    @pl.when(step > 0)
    def _():
        acc_ref[...] += part

    @pl.when(step == last)
    def _():
        for p in range(count):
            o_ref[ids_ref[p]] = acc_ref[p * TOK : (p + 1) * TOK, :].astype(BF16)


def upstream(ids, pieces, weights):
    far, rows, width = weights[0].shape
    near = GRID["fsdp"]
    depth = far * near * rows
    planes = 2
    steps = far // planes
    count = len(pieces)
    block = (planes, rows, width)
    return pl.pallas_call(
        upstream_kernel,
        grid_spec=pltpu.PrefetchScalarGridSpec(
            num_scalar_prefetch=1,
            grid=(steps,),
            in_specs=[pl.BlockSpec((TOK, depth // steps), lambda i, ids: (0, i))] * count
            + [pl.BlockSpec(block, lambda i, ids: (i, 0, 0))] * 3
            + [
                pl.BlockSpec(block, lambda i, ids: (jnp.minimum(i, steps // 2 - 1), 0, 0)),
                pl.BlockSpec(block, lambda i, ids: (jnp.maximum(i - steps // 2, 0), 0, 0)),
            ],
            out_specs=pl.BlockSpec((count, TOK, width), lambda i, ids: (0, 0, 0)),
            scratch_shapes=[
                pltpu.VMEM((count * TOK, width), F32),
                pltpu.VMEM((planes, near, rows, width), BF16),
            ],
        ),
        out_shape=jax.ShapeDtypeStruct((count, TOK, width), BF16),
        cost_estimate=pl.CostEstimate(
            flops=2 * count * TOK * width * depth,
            bytes_accessed=2 * (count * TOK * (depth + width) + depth * width),
            transcendentals=0,
        ),
        name="upstream",
    )(ids, *pieces, *weights)


def proj_kernel(ids_ref, *refs):
    pieces, refs = refs[:-9], refs[-9:]
    ot_ref, same_ref, next_ref, low_ref, high_ref, last_ref, side_ref, lhs_ref, out_ref = refs
    split = same_ref.shape[1]
    count = len(pieces)
    near = GRID["fsdp"]
    step = pl.program_id(0)
    middle = pl.num_programs(0) // 2

    @pl.when(step == 0)
    def _():
        for p in range(count):
            lhs_ref[:, p * TOK : (p + 1) * TOK] = ot_ref[ids_ref[p]]

    rows = jnp.concatenate([piece[...] for piece in pieces], 0)
    out_ref[...] = jnp.dot(lhs_ref[...], rows, preferred_element_type=F32).astype(BF16)

    def columns(offset):
        t = lax.rem(ids_ref[count + 1] + offset, near)
        return pl.ds(pl.multiple_of(t * TOK, TOK), TOK)

    def part(offset):
        return out_ref[:split, columns(offset)]

    for offset in range(near):
        side_ref[0, offset] = out_ref[split:, columns(offset)]

    same_ref[0] = part(0)
    next_ref[0] = part(1)
    last_ref[0] = part(3)

    @pl.when(step < middle)
    def _():
        low_ref[0] = part(2)

    @pl.when(step >= middle)
    def _():
        high_ref[0] = part(2)


def proj_terms(ids, pieces, ot):
    count, width, _ = ot.shape
    far, near = GRID["dp"], GRID["fsdp"]
    depth = pieces[0].shape[1]
    middle = far // 2
    split = width * 3 // 4
    block = (1, split, TOK)

    def plane(i, ids):
        return (i, 0, 0)

    full = jax.ShapeDtypeStruct((far, split, TOK), BF16)
    part = jax.ShapeDtypeStruct((middle, split, TOK), BF16)
    side = jax.ShapeDtypeStruct((far, near, width - split, TOK), BF16)
    return pl.pallas_call(
        proj_kernel,
        grid_spec=pltpu.PrefetchScalarGridSpec(
            num_scalar_prefetch=1,
            grid=(far,),
            in_specs=[pl.BlockSpec((TOK, near * TOK), lambda i, ids: (0, i))] * count
            + [pl.BlockSpec(ot.shape, lambda i, ids: (0, 0, 0))],
            out_specs=[
                pl.BlockSpec(block, plane),
                pl.BlockSpec(block, plane),
                pl.BlockSpec(block, lambda i, ids: (jnp.minimum(i, middle - 1), 0, 0)),
                pl.BlockSpec(block, lambda i, ids: (jnp.maximum(i - middle, 0), 0, 0)),
                pl.BlockSpec(block, plane),
                pl.BlockSpec((1, near, width - split, TOK), lambda i, ids: (i, 0, 0, 0)),
            ],
            scratch_shapes=[
                pltpu.VMEM((width, count * TOK), BF16),
                pltpu.VMEM((width, near * TOK), BF16),
            ],
        ),
        out_shape=[full, full, part, part, full, side],
        cost_estimate=pl.CostEstimate(
            flops=2 * count * TOK * width * depth,
            bytes_accessed=2 * (count * TOK * (depth + width) + depth * width),
            transcendentals=0,
        ),
        name="proj_terms",
    )(ids, *pieces, ot)


def join_kernel(low_ref, up_ref, high_ref, down_ref, low_out, high_out):
    low_out[...] = add(low_ref[...], up_ref[...])
    high_out[...] = add(high_ref[...], down_ref[...])


def join(low, up, high, down):
    planes, width, _ = up.shape
    block = (planes // 2, width, TOK)

    def front(i):
        return (i, 0, 0)

    def back(i):
        return (i + 2, 0, 0)

    return pl.pallas_call(
        join_kernel,
        grid=(2,),
        in_specs=[
            pl.BlockSpec(block, front),
            pl.BlockSpec(block, front),
            pl.BlockSpec(block, back),
            pl.BlockSpec(block, front),
        ],
        out_specs=[pl.BlockSpec(block, front), pl.BlockSpec(block, back)],
        out_shape=[jax.ShapeDtypeStruct(low.shape, BF16)] * 2,
        input_output_aliases={0: 0, 2: 1},
        cost_estimate=pl.CostEstimate(
            flops=2 * up.size, bytes_accessed=12 * up.size, transcendentals=0
        ),
        name="join",
    )(low, up, high, down)


def shift(x, axis, by):
    n = GRID[axis]
    return lax.ppermute(x, axis, [(i, (i + by) % n) for i in range(n)])


def add(a, b):
    return (a.astype(F32) + b.astype(F32)).astype(BF16)


def after(value, done):
    return lax.optimization_barrier((value, done))[0]


def swap(x, axis):
    return lax.all_to_all(x, axis, split_axis=0, concat_axis=0, tiled=True)


def hop(x, chips, core):
    pairs = [(i * 2 + c, ((i + chips) % 4) * 2 + (c ^ core)) for i in range(4) for c in range(2)]
    return lax.ppermute(x, "seq", pairs)


def per_device(
    query_rows, forward_key_rows, forward_value_rows, out_cotangent, proj_weight, sent_lengths
):
    place = lax.axis_index("seq").astype(jnp.int32)
    chip, core = place // 2, place % 2
    chips = (chip + jnp.array([0, 3, 1, 2], jnp.int32)) % 4 * 2
    ids = jnp.concatenate(
        [
            chips + core,
            chips + 1 - core,
            jnp.stack([lax.axis_index("dp"), lax.axis_index("fsdp")]).astype(jnp.int32),
        ]
    )
    targets = (chip + jnp.array([0, 1, 3, 2], jnp.int32)) % 4 * 2
    targets = jnp.concatenate([targets + core, targets + 1 - core])
    far = GRID["dp"] // 2
    half = TOK // 2
    own = out_cotangent[0]
    left, right = hop(own, 1, 0), hop(own, -1, 0)
    weight = jnp.broadcast_to(proj_weight, (2 * far, *proj_weight.shape))
    weight = swap(weight, "dp")
    packed = pack(targets, query_rows, forward_key_rows, forward_value_rows)
    paths = [(chips, flip) for flip in range(2) for chips in (0, 1, -1, 2)]
    packed = [packed[0]] + [hop(x, *path) for x, path in zip(packed[1:], paths[1:])]
    partner = hop(own, 0, 1)
    below, above = shift(weight, "fsdp", 1), shift(weight, "fsdp", -1)
    lo, hi = limits(sent_lengths[0], len(packed))
    across = [hop(left[:half], 1, 0), hop(right[half:], -1, 0)]
    across = jnp.concatenate(across, 0)
    output = attend(ids, packed, lo, hi)
    pieces = [own, left, right, across, partner]
    pieces += [hop(piece, 0, 1) for piece in (left, right, across)]
    same, following, low, high, before, side = proj_terms(ids, pieces, output)
    side = swap(side, "dp")
    up, down = shift(low, "fsdp", 1), shift(high, "fsdp", -1)
    below, above = after((below, above), low)
    ends = [shift(below[:far], "fsdp", 1), shift(above[far:], "fsdp", -1)]
    following, before = join(following, up, before, down)
    up, down = shift(following, "fsdp", 1), shift(before, "fsdp", -1)
    arriving = upstream(ids, pieces, [weight, below, above, *ends])
    grads = attend_grad(jnp.concatenate([ids, targets]), packed, arriving, lo, hi)
    side = after(side, arriving)
    first = (same.astype(F32) + up.astype(F32) + down.astype(F32)).astype(BF16)
    first = swap(first, "dp")
    grads = [grads[0]] + [hop(x, *path) for x, path in zip(grads[1:], paths[1:])]
    side = jnp.sum(side.astype(F32), axis=0)
    own_side, side = side[0], side.astype(BF16)
    side = [shift(side[by], "fsdp", by).astype(F32) for by in (1, 2, 3)]
    proj_grad = [jnp.sum(first.astype(F32), axis=0), own_side + side[0] + side[1] + side[2]]
    proj_grad = jnp.concatenate(proj_grad, 0).T.astype(BF16)
    query_grad, key_gradient, value_gradient = unpack(ids, grads)
    return (query_grad, key_gradient, value_gradient, proj_grad)


def solution(mesh):
    in_specs = (
        P(("dp", "fsdp"), "seq", None),
        P(("dp", "fsdp"), "seq", None),
        P(("dp", "fsdp"), "seq", None),
        P(("dp", "fsdp"), "seq", None),
        P(("dp", "fsdp"), "seq"),
        P(("dp", "fsdp"), None),
    )
    out_specs = (
        P(("dp", "fsdp"), "seq", None),
        P(("dp", "fsdp"), "seq", None),
        P(("dp", "fsdp"), "seq", None),
        P(("dp", "fsdp"), "seq"),
    )
    return jax.shard_map(
        per_device, mesh=mesh, in_specs=in_specs, out_specs=out_specs, check_vma=False
    )
```

```python
import math

import jax
import jax.numpy as jnp
from jax import lax
from jax.experimental import pallas as pl
from jax.experimental.pallas import tpu as pltpu
from jax.sharding import PartitionSpec as P

HEADS = 4
HEAD = 128
TOK = 128
KW = 448
FACTOR = 1.0 / math.sqrt(HEAD)
F32 = jnp.float32
BF16 = jnp.bfloat16
GROUP = 4
GRID = {"dp": 8, "fsdp": 4}


def window_start(i, blocks):
    return pl.multiple_of(jnp.clip(i * TOK - 256, 0, blocks * TOK - KW), 64)


def probs(i, start, q_ref, lo_ref, hi_ref, key, h0):
    q = jnp.concatenate(
        [q_ref[i, :, (h0 + j) * HEAD : (h0 + j + 1) * HEAD] for j in range(GROUP)], 0
    )
    s = lax.dot_general(key, q, (((1,), (1,)), ((), ())), preferred_element_type=F32)
    place = start + lax.broadcasted_iota(jnp.int32, (KW, GROUP * TOK), 0)
    lo = jnp.concatenate([lo_ref[i]] * GROUP, 1)
    hi = jnp.concatenate([hi_ref[i]] * GROUP, 1)
    p = jnp.where((place >= lo) & (place < hi), jnp.exp(s * FACTOR), 0.0)
    a = p * (1.0 / jnp.sum(p, axis=0, keepdims=True))
    return q, a


def assemble(ids_ref, pieces, q_ref, k_ref, v_ref):
    for p, piece in enumerate(pieces):
        b = ids_ref[p]
        rows = pl.ds(pl.multiple_of(b * TOK, TOK), TOK)
        q_ref[b] = piece[:, : HEADS * HEAD]
        k_ref[rows, :] = piece[:, HEADS * HEAD : (HEADS + 1) * HEAD]
        v_ref[rows, :] = piece[:, (HEADS + 1) * HEAD :]


def fwd_kernel(ids_ref, *refs):
    pieces, (lo_ref, hi_ref, o_ref, q_ref, k_ref, v_ref) = refs[:-6], refs[-6:]
    blocks = len(pieces)
    i = pl.program_id(0)

    @pl.when(i == 0)
    def _():
        assemble(ids_ref, pieces, q_ref, k_ref, v_ref)

    start = window_start(i, blocks)
    key = k_ref[pl.ds(start, KW), :]
    vt = v_ref[pl.ds(start, KW), :].T
    for h0 in range(0, HEADS, GROUP):
        _, a = probs(i, start, q_ref, lo_ref, hi_ref, key, h0)
        o = jnp.dot(vt, a.astype(BF16), preferred_element_type=F32).astype(BF16)
        for j in range(GROUP):
            o_ref[0, (h0 + j) * HEAD : (h0 + j + 1) * HEAD, :] = o[:, j * TOK : (j + 1) * TOK]


def bwd_kernel(ids_ref, *refs):
    blocks = (len(refs) - 9) // 2
    pieces, (u_ref, lo_ref, hi_ref) = refs[:blocks], refs[blocks : blocks + 3]
    homes, scratch = refs[blocks + 3 : -6], refs[-6:]
    o_ref, dk_ref, dv_ref, q_ref, k_ref, v_ref = scratch
    i = pl.program_id(0)

    @pl.when(i == 0)
    def _():
        assemble(ids_ref, pieces, q_ref, k_ref, v_ref)
        dk_ref[...] = jnp.zeros_like(dk_ref)
        dv_ref[...] = jnp.zeros_like(dv_ref)

    start = window_start(i, blocks)
    key = k_ref[pl.ds(start, KW), :]
    val = v_ref[pl.ds(start, KW), :]
    kt = key.T
    dk = None
    for h0 in range(0, HEADS, GROUP):
        q, a = probs(i, start, q_ref, lo_ref, hi_ref, key, h0)
        u = jnp.concatenate(
            [u_ref[i, :, (h0 + j) * HEAD : (h0 + j + 1) * HEAD] for j in range(GROUP)], 0
        )
        g = lax.dot_general(val, u, (((1,), (1,)), ((), ())), preferred_element_type=F32)
        delta = jnp.sum(a * g, axis=0, keepdims=True)
        ds = (a * (g - delta) * FACTOR).astype(BF16)
        dq = jnp.dot(kt, ds, preferred_element_type=F32)
        for j in range(GROUP):
            o_ref[i, :, (h0 + j) * HEAD : (h0 + j + 1) * HEAD] = dq[
                :, j * TOK : (j + 1) * TOK
            ].T.astype(BF16)
        dkh = jnp.dot(ds, q, preferred_element_type=F32)
        dvh = jnp.dot(a.astype(BF16), u, preferred_element_type=F32)
        dk, dv = (dkh, dvh) if dk is None else (dk + dkh, dv + dvh)
    dk_ref[pl.ds(start, KW), :] += dk
    dv_ref[pl.ds(start, KW), :] += dv

    @pl.when(i == blocks - 1)
    def _():
        for p, home in enumerate(homes):
            b = ids_ref[blocks + 2 + p]
            rows = pl.ds(pl.multiple_of(b * TOK, TOK), TOK)
            home[:, : HEADS * HEAD] = o_ref[b]
            home[:, HEADS * HEAD : (HEADS + 1) * HEAD] = dk_ref[rows, :].astype(BF16)
            home[:, (HEADS + 1) * HEAD :] = dv_ref[rows, :].astype(BF16)


def whole(shape):
    return pl.BlockSpec(shape, lambda i, ids: (0,) * len(shape))


def limits(sent_lengths, blocks):
    number = sent_lengths.shape[0]
    order = jnp.arange(number, dtype=jnp.int32)
    ends = jnp.sum(jnp.where(order[None, :] <= order[:, None], sent_lengths[None, :], 0), axis=1)
    places = jnp.arange(blocks * TOK, dtype=jnp.int32)
    sentence = jnp.sum((places[:, None] >= ends[None, :]).astype(jnp.int32), axis=1)
    lo = jnp.sum(
        jnp.where(order[None, :] + 3 < sentence[:, None], sent_lengths[None, :], 0), axis=1
    )
    hi = jnp.sum(jnp.where(order[None, :] <= sentence[:, None], sent_lengths[None, :], 0), axis=1)
    return lo.reshape(blocks, 1, TOK), hi.reshape(blocks, 1, TOK)


def head_scratch(blocks):
    keys = pltpu.VMEM((blocks * TOK, HEAD), BF16)
    return [pltpu.VMEM((blocks, TOK, HEADS * HEAD), BF16), keys, keys]


def attend(ids, pieces, lo, hi):
    blocks = len(pieces)
    pairs = blocks * TOK * KW * HEADS
    return pl.pallas_call(
        fwd_kernel,
        grid_spec=pltpu.PrefetchScalarGridSpec(
            num_scalar_prefetch=1,
            grid=(blocks,),
            in_specs=[whole(x.shape) for x in (*pieces, lo, hi)],
            out_specs=pl.BlockSpec((1, HEADS * HEAD, TOK), lambda i, ids: (i, 0, 0)),
            scratch_shapes=head_scratch(blocks),
        ),
        out_shape=jax.ShapeDtypeStruct((blocks, HEADS * HEAD, TOK), BF16),
        cost_estimate=pl.CostEstimate(
            flops=4 * pairs * HEAD,
            bytes_accessed=4 * blocks * pieces[0].size,
            transcendentals=pairs,
        ),
        name="attend",
    )(ids, *pieces, lo, hi)


def attend_grad(ids, pieces, u, lo, hi):
    blocks = len(pieces)
    pairs = blocks * TOK * KW * HEADS
    shape = pieces[0].shape
    return pl.pallas_call(
        bwd_kernel,
        grid_spec=pltpu.PrefetchScalarGridSpec(
            num_scalar_prefetch=1,
            grid=(blocks,),
            in_specs=[whole(x.shape) for x in (*pieces, u, lo, hi)],
            out_specs=[whole(shape)] * blocks,
            scratch_shapes=[pltpu.VMEM((blocks, TOK, HEADS * HEAD), BF16)]
            + [pltpu.VMEM((blocks * TOK, HEAD), F32)] * 2
            + head_scratch(blocks),
        ),
        out_shape=[jax.ShapeDtypeStruct(shape, BF16)] * blocks,
        cost_estimate=pl.CostEstimate(
            flops=10 * pairs * HEAD,
            bytes_accessed=6 * blocks * pieces[0].size,
            transcendentals=pairs,
        ),
        name="attend_grad",
    )(ids, *pieces, u, lo, hi)


def pack_kernel(ids_ref, q_ref, k_ref, v_ref, *o_refs):
    wide = HEADS * HEAD
    for p, o_ref in enumerate(o_refs):
        g = ids_ref[p]
        heads = pl.ds(pl.multiple_of(g * HEAD, HEAD), HEAD)
        o_ref[:, :wide] = q_ref[0, :, pl.ds(pl.multiple_of(g * wide, wide), wide)]
        o_ref[:, wide : wide + HEAD] = k_ref[0, :, heads]
        o_ref[:, wide + HEAD :] = v_ref[0, :, heads]


def pack(ids, q, k, v):
    groups = k.shape[2] // HEAD
    width = (HEADS + 2) * HEAD
    return pl.pallas_call(
        pack_kernel,
        grid_spec=pltpu.PrefetchScalarGridSpec(
            num_scalar_prefetch=1,
            grid=(1,),
            in_specs=[whole(x.shape) for x in (q, k, v)],
            out_specs=[whole((TOK, width))] * groups,
        ),
        out_shape=[jax.ShapeDtypeStruct((TOK, width), BF16)] * groups,
        cost_estimate=pl.CostEstimate(flops=0, bytes_accessed=6 * q.size, transcendentals=0),
        name="pack",
    )(ids, q, k, v)


def unpack_kernel(ids_ref, *refs):
    wide = HEADS * HEAD
    pieces, (q_ref, k_ref, v_ref) = refs[:-3], refs[-3:]
    for p, piece in enumerate(pieces):
        g = ids_ref[p]
        heads = pl.ds(pl.multiple_of(g * HEAD, HEAD), HEAD)
        q_ref[0, :, pl.ds(pl.multiple_of(g * wide, wide), wide)] = piece[:, :wide]
        k_ref[0, :, heads] = piece[:, wide : wide + HEAD]
        v_ref[0, :, heads] = piece[:, wide + HEAD :]


def unpack(ids, pieces):
    groups = len(pieces)
    shapes = [(1, TOK, groups * part) for part in (HEADS * HEAD, HEAD, HEAD)]
    return pl.pallas_call(
        unpack_kernel,
        grid_spec=pltpu.PrefetchScalarGridSpec(
            num_scalar_prefetch=1,
            grid=(1,),
            in_specs=[whole(x.shape) for x in pieces],
            out_specs=[whole(shape) for shape in shapes],
        ),
        out_shape=[jax.ShapeDtypeStruct(shape, BF16) for shape in shapes],
        cost_estimate=pl.CostEstimate(
            flops=0, bytes_accessed=4 * groups * pieces[0].size, transcendentals=0
        ),
        name="unpack",
    )(ids, *pieces)


def gathered_rows(ids_ref, pieces, offsets):
    near = GRID["fsdp"]
    planes = pieces[0].shape[1] // (near * TOK)
    turn = ids_ref[len(pieces) + 1]
    starts = [
        pl.multiple_of((plane * near + lax.rem(turn + offset, near)) * TOK, TOK)
        for offset in offsets
        for plane in range(planes)
    ]
    return jnp.concatenate(
        [
            jnp.concatenate([piece[:, pl.ds(start, TOK)] for start in starts], 1)
            for piece in pieces
        ],
        0,
    )


def most_kernel(ids_ref, *refs):
    pieces, (mine_ref, below_ref, above_ref, o_ref) = refs[:-4], refs[-4:]
    near = GRID["fsdp"]
    rows = gathered_rows(ids_ref, pieces, (0, near - 1, 1))
    width = mine_ref.shape[2]
    weight = jnp.concatenate(
        [x[...].reshape(-1, width) for x in (mine_ref, below_ref, above_ref)], 0
    )
    part = jnp.dot(rows, weight, preferred_element_type=F32)
    first = pl.program_id(0) == 0

    @pl.when(first)
    def _():
        o_ref[...] = part

    @pl.when(jnp.logical_not(first))
    def _():
        o_ref[...] += part


def rest_kernel(ids_ref, *refs):
    pieces, (low_ref, high_ref, sum_ref, o_ref, acc_ref) = refs[:-5], refs[-5:]
    step = pl.program_id(0)
    last = pl.num_programs(0) - 1
    rows = gathered_rows(ids_ref, pieces, (2,))
    weight = jnp.where(step * 2 <= last, low_ref[...], high_ref[...])
    part = jnp.dot(rows, weight.reshape(-1, weight.shape[2]), preferred_element_type=F32)

    @pl.when(step == 0)
    def _():
        acc_ref[...] = sum_ref[...] + part

    @pl.when(step > 0)
    def _():
        acc_ref[...] += part

    @pl.when(step == last)
    def _():
        for p in range(len(pieces)):
            o_ref[ids_ref[p]] = acc_ref[p * TOK : (p + 1) * TOK, :].astype(BF16)


PLANES = 2


def chunk_specs(pieces):
    near = GRID["fsdp"]
    return [pl.BlockSpec((TOK, PLANES * near * TOK), lambda i, ids: (0, i))] * len(pieces)


def upstream_most(ids, pieces, weights):
    far, rows, width = weights[0].shape
    count = len(pieces)
    tokens = count * TOK
    depth = 3 * far * rows
    return pl.pallas_call(
        most_kernel,
        grid_spec=pltpu.PrefetchScalarGridSpec(
            num_scalar_prefetch=1,
            grid=(far // PLANES,),
            in_specs=chunk_specs(pieces)
            + [pl.BlockSpec((PLANES, rows, width), lambda i, ids: (i, 0, 0))] * 3,
            out_specs=whole((tokens, width)),
        ),
        out_shape=jax.ShapeDtypeStruct((tokens, width), F32),
        cost_estimate=pl.CostEstimate(
            flops=2 * tokens * width * depth,
            bytes_accessed=2 * (tokens * (depth + 2 * width) + depth * width),
            transcendentals=0,
        ),
        name="upstream_most",
    )(ids, *pieces, *weights)


def upstream_rest(ids, pieces, ends, sums):
    middle, rows, width = ends[0].shape
    count = len(pieces)
    steps = 2 * middle // PLANES
    block = (PLANES, rows, width)
    depth = 2 * middle * rows
    return pl.pallas_call(
        rest_kernel,
        grid_spec=pltpu.PrefetchScalarGridSpec(
            num_scalar_prefetch=1,
            grid=(steps,),
            in_specs=chunk_specs(pieces)
            + [
                pl.BlockSpec(block, lambda i, ids: (jnp.minimum(i, steps // 2 - 1), 0, 0)),
                pl.BlockSpec(block, lambda i, ids: (jnp.maximum(i - steps // 2, 0), 0, 0)),
                whole(sums.shape),
            ],
            out_specs=whole((count, TOK, width)),
            scratch_shapes=[pltpu.VMEM(sums.shape, F32)],
        ),
        out_shape=jax.ShapeDtypeStruct((count, TOK, width), BF16),
        cost_estimate=pl.CostEstimate(
            flops=2 * count * TOK * width * depth,
            bytes_accessed=2 * count * TOK * (4 * depth + 3 * width),
            transcendentals=0,
        ),
        name="upstream_rest",
    )(ids, *pieces, *ends, sums)


def proj_kernel(ids_ref, *refs):
    pieces, refs = refs[:-8], refs[-8:]
    ot_ref, same_ref, next_ref, low_ref, high_ref, last_ref, lhs_ref, out_ref = refs
    count = len(pieces)
    near = GRID["fsdp"]
    step = pl.program_id(0)
    middle = pl.num_programs(0) // 2

    @pl.when(step == 0)
    def _():
        for p in range(count):
            lhs_ref[:, p * TOK : (p + 1) * TOK] = ot_ref[ids_ref[p]]

    rows = jnp.concatenate([piece[...] for piece in pieces], 0)
    out_ref[...] = jnp.dot(lhs_ref[...], rows, preferred_element_type=F32).astype(BF16)

    def part(offset):
        t = lax.rem(ids_ref[count + 1] + offset, near)
        return out_ref[:, pl.ds(pl.multiple_of(t * TOK, TOK), TOK)]

    same_ref[0] = part(0)
    next_ref[0] = part(1)
    last_ref[0] = part(3)

    @pl.when(step < middle)
    def _():
        low_ref[0] = part(2)

    @pl.when(step >= middle)
    def _():
        high_ref[0] = part(2)


def proj_terms(ids, pieces, ot):
    count, width, _ = ot.shape
    far, near = GRID["dp"], GRID["fsdp"]
    depth = pieces[0].shape[1]
    middle = far // 2
    block = (1, width, TOK)

    def plane(i, ids):
        return (i, 0, 0)

    full = jax.ShapeDtypeStruct((far, width, TOK), BF16)
    part = jax.ShapeDtypeStruct((middle, width, TOK), BF16)
    return pl.pallas_call(
        proj_kernel,
        grid_spec=pltpu.PrefetchScalarGridSpec(
            num_scalar_prefetch=1,
            grid=(far,),
            in_specs=[pl.BlockSpec((TOK, near * TOK), lambda i, ids: (0, i))] * count
            + [pl.BlockSpec(ot.shape, lambda i, ids: (0, 0, 0))],
            out_specs=[
                pl.BlockSpec(block, plane),
                pl.BlockSpec(block, plane),
                pl.BlockSpec(block, lambda i, ids: (jnp.minimum(i, middle - 1), 0, 0)),
                pl.BlockSpec(block, lambda i, ids: (jnp.maximum(i - middle, 0), 0, 0)),
                pl.BlockSpec(block, plane),
            ],
            scratch_shapes=[
                pltpu.VMEM((width, count * TOK), BF16),
                pltpu.VMEM((width, near * TOK), BF16),
            ],
        ),
        out_shape=[full, full, part, part, full],
        cost_estimate=pl.CostEstimate(
            flops=2 * count * TOK * width * depth,
            bytes_accessed=2 * (count * TOK * (depth + width) + depth * width),
            transcendentals=0,
        ),
        name="proj_terms",
    )(ids, *pieces, ot)


def join_kernel(low_ref, up_ref, high_ref, down_ref, low_out, high_out):
    low_out[...] = add(low_ref[...], up_ref[...])
    high_out[...] = add(high_ref[...], down_ref[...])


def join(low, up, high, down):
    planes, width, _ = up.shape
    block = (planes // 2, width, TOK)

    def front(i):
        return (i, 0, 0)

    def back(i):
        return (i + 2, 0, 0)

    return pl.pallas_call(
        join_kernel,
        grid=(2,),
        in_specs=[
            pl.BlockSpec(block, front),
            pl.BlockSpec(block, front),
            pl.BlockSpec(block, back),
            pl.BlockSpec(block, front),
        ],
        out_specs=[pl.BlockSpec(block, front), pl.BlockSpec(block, back)],
        out_shape=[jax.ShapeDtypeStruct(low.shape, BF16)] * 2,
        input_output_aliases={0: 0, 2: 1},
        cost_estimate=pl.CostEstimate(
            flops=2 * up.size, bytes_accessed=12 * up.size, transcendentals=0
        ),
        name="join",
    )(low, up, high, down)


def shift(x, axis, by):
    n = GRID[axis]
    return lax.ppermute(x, axis, [(i, (i + by) % n) for i in range(n)])


def add(a, b):
    return (a.astype(F32) + b.astype(F32)).astype(BF16)


def after(value, done):
    return lax.optimization_barrier((value, done))[0]


def swap(x, axis):
    return lax.all_to_all(x, axis, split_axis=0, concat_axis=0, tiled=True)


def hop(x, chips, core):
    pairs = [(i * 2 + c, ((i + chips) % 4) * 2 + (c ^ core)) for i in range(4) for c in range(2)]
    return lax.ppermute(x, "seq", pairs)


def per_device(
    query_rows, forward_key_rows, forward_value_rows, out_cotangent, proj_weight, sent_lengths
):
    place = lax.axis_index("seq").astype(jnp.int32)
    chip, core = place // 2, place % 2
    chips = (chip + jnp.array([0, 3, 1, 2], jnp.int32)) % 4 * 2
    ids = jnp.concatenate(
        [
            chips + core,
            chips + 1 - core,
            jnp.stack([lax.axis_index("dp"), lax.axis_index("fsdp")]).astype(jnp.int32),
        ]
    )
    targets = (chip + jnp.array([0, 1, 3, 2], jnp.int32)) % 4 * 2
    targets = jnp.concatenate([targets + core, targets + 1 - core])
    far = GRID["dp"] // 2
    half = TOK // 2
    own = out_cotangent[0]
    left, right = hop(own, 1, 0), hop(own, -1, 0)
    weight = jnp.broadcast_to(proj_weight, (2 * far, *proj_weight.shape))
    weight = swap(weight, "dp")
    packed = pack(targets, query_rows, forward_key_rows, forward_value_rows)
    paths = [(chips, flip) for flip in range(2) for chips in (0, 1, -1, 2)]
    packed = [packed[0]] + [hop(x, *path) for x, path in zip(packed[1:], paths[1:])]
    partner = hop(own, 0, 1)
    below, above = shift(weight, "fsdp", 1), shift(weight, "fsdp", -1)
    lo, hi = limits(sent_lengths[0], len(packed))
    across = [hop(left[:half], 1, 0), hop(right[half:], -1, 0)]
    across = jnp.concatenate(across, 0)
    output = attend(ids, packed, lo, hi)
    pieces = [own, left, right, across, partner]
    pieces += [hop(piece, 0, 1) for piece in (left, right, across)]
    same, following, low, high, before = proj_terms(ids, pieces, output)
    up, down = shift(low, "fsdp", 1), shift(high, "fsdp", -1)
    below, above = after((below, above), low)
    ends = [shift(below[:far], "fsdp", 1), shift(above[far:], "fsdp", -1)]
    sums = upstream_most(ids, pieces, [weight, below, above])
    following, before = join(following, up, before, down)
    up, down = shift(following, "fsdp", 1), shift(before, "fsdp", -1)
    arriving = upstream_rest(ids, pieces, ends, sums)
    grads = attend_grad(jnp.concatenate([ids, targets]), packed, arriving, lo, hi)
    up, down = after((up, down), grads[0])
    first = (same.astype(F32) + up.astype(F32) + down.astype(F32)).astype(BF16)
    first = swap(first, "dp")
    grads = [grads[0]] + [hop(x, *path) for x, path in zip(grads[1:], paths[1:])]
    proj_grad = jnp.sum(first.astype(F32), axis=0).T.astype(BF16)
    query_grad, key_gradient, value_gradient = unpack(ids, grads)
    return (query_grad, key_gradient, value_gradient, proj_grad)


def solution(mesh):
    in_specs = (
        P(("dp", "fsdp"), "seq", None),
        P(("dp", "fsdp"), "seq", None),
        P(("dp", "fsdp"), "seq", None),
        P(("dp", "fsdp"), "seq", None),
        P(("dp", "fsdp"), "seq"),
        P(("dp", "fsdp"), None),
    )
    out_specs = (
        P(("dp", "fsdp"), "seq", None),
        P(("dp", "fsdp"), "seq", None),
        P(("dp", "fsdp"), "seq", None),
        P(("dp", "fsdp"), "seq"),
    )
    return jax.shard_map(
        per_device, mesh=mesh, in_specs=in_specs, out_specs=out_specs, check_vma=False
    )
```

```python
import math

import jax
import jax.numpy as jnp
from jax import lax
from jax.experimental import pallas as pl
from jax.experimental.pallas import tpu as pltpu
from jax.sharding import PartitionSpec as P

HEADS = 4
HEAD = 128
TOK = 128
KW = 448
FACTOR = 1.0 / math.sqrt(HEAD)
F32 = jnp.float32
BF16 = jnp.bfloat16
GROUP = 4
GRID = {"dp": 8, "fsdp": 4}


def window_start(i, blocks):
    return pl.multiple_of(jnp.clip(i * TOK - 256, 0, blocks * TOK - KW), 64)


def probs(i, start, q_ref, lo_ref, hi_ref, key, h0):
    q = jnp.concatenate(
        [q_ref[i, :, (h0 + j) * HEAD : (h0 + j + 1) * HEAD] for j in range(GROUP)], 0
    )
    s = lax.dot_general(key, q, (((1,), (1,)), ((), ())), preferred_element_type=F32)
    place = start + lax.broadcasted_iota(jnp.int32, (KW, GROUP * TOK), 0)
    lo = jnp.concatenate([lo_ref[i]] * GROUP, 1)
    hi = jnp.concatenate([hi_ref[i]] * GROUP, 1)
    p = jnp.where((place >= lo) & (place < hi), jnp.exp(s * FACTOR), 0.0)
    a = p * (1.0 / jnp.sum(p, axis=0, keepdims=True))
    return q, a


def assemble(ids_ref, pieces, q_ref, k_ref, v_ref):
    for p, piece in enumerate(pieces):
        b = ids_ref[p]
        rows = pl.ds(pl.multiple_of(b * TOK, TOK), TOK)
        q_ref[b] = piece[:, : HEADS * HEAD]
        k_ref[rows, :] = piece[:, HEADS * HEAD : (HEADS + 1) * HEAD]
        v_ref[rows, :] = piece[:, (HEADS + 1) * HEAD :]


def fwd_kernel(ids_ref, *refs):
    pieces, (lo_ref, hi_ref, o_ref, q_ref, k_ref, v_ref) = refs[:-6], refs[-6:]
    blocks = len(pieces)
    i = pl.program_id(0)

    @pl.when(i == 0)
    def _():
        assemble(ids_ref, pieces, q_ref, k_ref, v_ref)

    start = window_start(i, blocks)
    key = k_ref[pl.ds(start, KW), :]
    vt = v_ref[pl.ds(start, KW), :].T
    for h0 in range(0, HEADS, GROUP):
        _, a = probs(i, start, q_ref, lo_ref, hi_ref, key, h0)
        o = jnp.dot(vt, a.astype(BF16), preferred_element_type=F32).astype(BF16)
        for j in range(GROUP):
            o_ref[0, (h0 + j) * HEAD : (h0 + j + 1) * HEAD, :] = o[:, j * TOK : (j + 1) * TOK]


def bwd_kernel(ids_ref, *refs):
    blocks = (len(refs) - 9) // 2
    pieces, (u_ref, lo_ref, hi_ref) = refs[:blocks], refs[blocks : blocks + 3]
    homes, scratch = refs[blocks + 3 : -6], refs[-6:]
    o_ref, dk_ref, dv_ref, q_ref, k_ref, v_ref = scratch
    i = pl.program_id(0)

    @pl.when(i == 0)
    def _():
        assemble(ids_ref, pieces, q_ref, k_ref, v_ref)
        dk_ref[...] = jnp.zeros_like(dk_ref)
        dv_ref[...] = jnp.zeros_like(dv_ref)

    start = window_start(i, blocks)
    key = k_ref[pl.ds(start, KW), :]
    val = v_ref[pl.ds(start, KW), :]
    kt = key.T
    dk = None
    for h0 in range(0, HEADS, GROUP):
        q, a = probs(i, start, q_ref, lo_ref, hi_ref, key, h0)
        u = jnp.concatenate(
            [u_ref[i, :, (h0 + j) * HEAD : (h0 + j + 1) * HEAD] for j in range(GROUP)], 0
        )
        g = lax.dot_general(val, u, (((1,), (1,)), ((), ())), preferred_element_type=F32)
        delta = jnp.sum(a * g, axis=0, keepdims=True)
        ds = (a * (g - delta) * FACTOR).astype(BF16)
        dq = jnp.dot(kt, ds, preferred_element_type=F32)
        for j in range(GROUP):
            o_ref[i, :, (h0 + j) * HEAD : (h0 + j + 1) * HEAD] = dq[
                :, j * TOK : (j + 1) * TOK
            ].T.astype(BF16)
        dkh = jnp.dot(ds, q, preferred_element_type=F32)
        dvh = jnp.dot(a.astype(BF16), u, preferred_element_type=F32)
        dk, dv = (dkh, dvh) if dk is None else (dk + dkh, dv + dvh)
    dk_ref[pl.ds(start, KW), :] += dk
    dv_ref[pl.ds(start, KW), :] += dv

    @pl.when(i == blocks - 1)
    def _():
        for p, home in enumerate(homes):
            b = ids_ref[blocks + 2 + p]
            rows = pl.ds(pl.multiple_of(b * TOK, TOK), TOK)
            home[:, : HEADS * HEAD] = o_ref[b]
            home[:, HEADS * HEAD : (HEADS + 1) * HEAD] = dk_ref[rows, :].astype(BF16)
            home[:, (HEADS + 1) * HEAD :] = dv_ref[rows, :].astype(BF16)


def whole(shape):
    return pl.BlockSpec(shape, lambda i, ids: (0,) * len(shape))


def limits(sent_lengths, blocks):
    number = sent_lengths.shape[0]
    order = jnp.arange(number, dtype=jnp.int32)
    ends = jnp.sum(jnp.where(order[None, :] <= order[:, None], sent_lengths[None, :], 0), axis=1)
    places = jnp.arange(blocks * TOK, dtype=jnp.int32)
    sentence = jnp.sum((places[:, None] >= ends[None, :]).astype(jnp.int32), axis=1)
    lo = jnp.sum(
        jnp.where(order[None, :] + 3 < sentence[:, None], sent_lengths[None, :], 0), axis=1
    )
    hi = jnp.sum(jnp.where(order[None, :] <= sentence[:, None], sent_lengths[None, :], 0), axis=1)
    return lo.reshape(blocks, 1, TOK), hi.reshape(blocks, 1, TOK)


def head_scratch(blocks):
    keys = pltpu.VMEM((blocks * TOK, HEAD), BF16)
    return [pltpu.VMEM((blocks, TOK, HEADS * HEAD), BF16), keys, keys]


def attend(ids, pieces, lo, hi):
    blocks = len(pieces)
    pairs = blocks * TOK * KW * HEADS
    return pl.pallas_call(
        fwd_kernel,
        grid_spec=pltpu.PrefetchScalarGridSpec(
            num_scalar_prefetch=1,
            grid=(blocks,),
            in_specs=[whole(x.shape) for x in (*pieces, lo, hi)],
            out_specs=pl.BlockSpec((1, HEADS * HEAD, TOK), lambda i, ids: (i, 0, 0)),
            scratch_shapes=head_scratch(blocks),
        ),
        out_shape=jax.ShapeDtypeStruct((blocks, HEADS * HEAD, TOK), BF16),
        cost_estimate=pl.CostEstimate(
            flops=4 * pairs * HEAD,
            bytes_accessed=4 * blocks * pieces[0].size,
            transcendentals=pairs,
        ),
        name="attend",
    )(ids, *pieces, lo, hi)


def attend_grad(ids, pieces, u, lo, hi):
    blocks = len(pieces)
    pairs = blocks * TOK * KW * HEADS
    shape = pieces[0].shape
    return pl.pallas_call(
        bwd_kernel,
        grid_spec=pltpu.PrefetchScalarGridSpec(
            num_scalar_prefetch=1,
            grid=(blocks,),
            in_specs=[whole(x.shape) for x in (*pieces, u, lo, hi)],
            out_specs=[whole(shape)] * blocks,
            scratch_shapes=[pltpu.VMEM((blocks, TOK, HEADS * HEAD), BF16)]
            + [pltpu.VMEM((blocks * TOK, HEAD), F32)] * 2
            + head_scratch(blocks),
        ),
        out_shape=[jax.ShapeDtypeStruct(shape, BF16)] * blocks,
        cost_estimate=pl.CostEstimate(
            flops=10 * pairs * HEAD,
            bytes_accessed=6 * blocks * pieces[0].size,
            transcendentals=pairs,
        ),
        name="attend_grad",
    )(ids, *pieces, u, lo, hi)


def pack_kernel(ids_ref, q_ref, k_ref, v_ref, *o_refs):
    wide = HEADS * HEAD
    for p, o_ref in enumerate(o_refs):
        g = ids_ref[p]
        heads = pl.ds(pl.multiple_of(g * HEAD, HEAD), HEAD)
        o_ref[:, :wide] = q_ref[0, :, pl.ds(pl.multiple_of(g * wide, wide), wide)]
        o_ref[:, wide : wide + HEAD] = k_ref[0, :, heads]
        o_ref[:, wide + HEAD :] = v_ref[0, :, heads]


def pack(ids, q, k, v):
    groups = k.shape[2] // HEAD
    width = (HEADS + 2) * HEAD
    return pl.pallas_call(
        pack_kernel,
        grid_spec=pltpu.PrefetchScalarGridSpec(
            num_scalar_prefetch=1,
            grid=(1,),
            in_specs=[whole(x.shape) for x in (q, k, v)],
            out_specs=[whole((TOK, width))] * groups,
        ),
        out_shape=[jax.ShapeDtypeStruct((TOK, width), BF16)] * groups,
        cost_estimate=pl.CostEstimate(flops=0, bytes_accessed=6 * q.size, transcendentals=0),
        name="pack",
    )(ids, q, k, v)


def unpack_kernel(ids_ref, *refs):
    wide = HEADS * HEAD
    pieces, (q_ref, k_ref, v_ref) = refs[:-3], refs[-3:]
    for p, piece in enumerate(pieces):
        g = ids_ref[p]
        heads = pl.ds(pl.multiple_of(g * HEAD, HEAD), HEAD)
        q_ref[0, :, pl.ds(pl.multiple_of(g * wide, wide), wide)] = piece[:, :wide]
        k_ref[0, :, heads] = piece[:, wide : wide + HEAD]
        v_ref[0, :, heads] = piece[:, wide + HEAD :]


def unpack(ids, pieces):
    groups = len(pieces)
    shapes = [(1, TOK, groups * part) for part in (HEADS * HEAD, HEAD, HEAD)]
    return pl.pallas_call(
        unpack_kernel,
        grid_spec=pltpu.PrefetchScalarGridSpec(
            num_scalar_prefetch=1,
            grid=(1,),
            in_specs=[whole(x.shape) for x in pieces],
            out_specs=[whole(shape) for shape in shapes],
        ),
        out_shape=[jax.ShapeDtypeStruct(shape, BF16) for shape in shapes],
        cost_estimate=pl.CostEstimate(
            flops=0, bytes_accessed=4 * groups * pieces[0].size, transcendentals=0
        ),
        name="unpack",
    )(ids, *pieces)


def gathered_rows(ids_ref, pieces, offsets):
    near = GRID["fsdp"]
    planes = pieces[0].shape[1] // (near * TOK)
    turn = ids_ref[len(pieces) + 1]
    starts = [
        pl.multiple_of((plane * near + lax.rem(turn + offset, near)) * TOK, TOK)
        for offset in offsets
        for plane in range(planes)
    ]
    return jnp.concatenate(
        [
            jnp.concatenate([piece[:, pl.ds(start, TOK)] for start in starts], 1)
            for piece in pieces
        ],
        0,
    )


def most_kernel(ids_ref, *refs):
    pieces, (mine_ref, below_ref, above_ref, o_ref, left_ref) = refs[:-5], refs[-5:]
    near = GRID["fsdp"]
    left_ref[...] = gathered_rows(ids_ref, pieces, (2,))
    rows = gathered_rows(ids_ref, pieces, (0, near - 1, 1))
    width = mine_ref.shape[2]
    weight = jnp.concatenate(
        [x[...].reshape(-1, width) for x in (mine_ref, below_ref, above_ref)], 0
    )
    part = jnp.dot(rows, weight, preferred_element_type=F32)
    first = pl.program_id(0) == 0

    @pl.when(first)
    def _():
        o_ref[...] = part

    @pl.when(jnp.logical_not(first))
    def _():
        o_ref[...] += part


def rest_kernel(ids_ref, rows_ref, low_ref, high_ref, sum_ref, o_ref):
    width = low_ref.shape[2]
    weight = jnp.concatenate([x[...].reshape(-1, width) for x in (low_ref, high_ref)], 0)
    total = sum_ref[...] + jnp.dot(rows_ref[...], weight, preferred_element_type=F32)
    count = rows_ref.shape[0] // TOK
    first = pl.program_id(0) * count
    for p in range(count):
        o_ref[ids_ref[first + p]] = total[p * TOK : (p + 1) * TOK, :].astype(BF16)


PLANES = 2


def chunk_specs(pieces):
    near = GRID["fsdp"]
    return [pl.BlockSpec((TOK, PLANES * near * TOK), lambda i, ids: (0, i))] * len(pieces)


def upstream_most(ids, pieces, weights):
    far, rows, width = weights[0].shape
    count = len(pieces)
    tokens = count * TOK
    depth = 3 * far * rows
    return pl.pallas_call(
        most_kernel,
        grid_spec=pltpu.PrefetchScalarGridSpec(
            num_scalar_prefetch=1,
            grid=(far // PLANES,),
            in_specs=chunk_specs(pieces)
            + [pl.BlockSpec((PLANES, rows, width), lambda i, ids: (i, 0, 0))] * 3,
            out_specs=[
                whole((tokens, width)),
                pl.BlockSpec((tokens, PLANES * TOK), lambda i, ids: (0, i)),
            ],
        ),
        out_shape=[
            jax.ShapeDtypeStruct((tokens, width), F32),
            jax.ShapeDtypeStruct((tokens, far * TOK), BF16),
        ],
        cost_estimate=pl.CostEstimate(
            flops=2 * tokens * width * depth,
            bytes_accessed=2 * (tokens * (depth + 2 * width) + depth * width),
            transcendentals=0,
        ),
        name="upstream_most",
    )(ids, *pieces, *weights)


def upstream_rest(ids, rows, ends, sums):
    tokens, depth = rows.shape
    width = sums.shape[1]
    steps = 2
    return pl.pallas_call(
        rest_kernel,
        grid_spec=pltpu.PrefetchScalarGridSpec(
            num_scalar_prefetch=1,
            grid=(steps,),
            in_specs=[
                pl.BlockSpec((tokens // steps, depth), lambda i, ids: (i, 0)),
                whole(ends[0].shape),
                whole(ends[1].shape),
                pl.BlockSpec((tokens // steps, width), lambda i, ids: (i, 0)),
            ],
            out_specs=whole((tokens // TOK, TOK, width)),
        ),
        out_shape=jax.ShapeDtypeStruct((tokens // TOK, TOK, width), BF16),
        cost_estimate=pl.CostEstimate(
            flops=2 * tokens * width * depth,
            bytes_accessed=2 * (tokens * (depth + 3 * width) + depth * width),
            transcendentals=0,
        ),
        name="upstream_rest",
    )(ids, rows, *ends, sums)


def proj_kernel(ids_ref, *refs):
    pieces, refs = refs[:-8], refs[-8:]
    ot_ref, same_ref, next_ref, low_ref, high_ref, last_ref, lhs_ref, out_ref = refs
    count = len(pieces)
    near = GRID["fsdp"]
    step = pl.program_id(0)
    middle = pl.num_programs(0) // 2

    @pl.when(step == 0)
    def _():
        for p in range(count):
            lhs_ref[:, p * TOK : (p + 1) * TOK] = ot_ref[ids_ref[p]]

    rows = jnp.concatenate([piece[...] for piece in pieces], 0)
    out_ref[...] = jnp.dot(lhs_ref[...], rows, preferred_element_type=F32).astype(BF16)

    def part(offset):
        t = lax.rem(ids_ref[count + 1] + offset, near)
        return out_ref[:, pl.ds(pl.multiple_of(t * TOK, TOK), TOK)]

    same_ref[0] = part(0)
    next_ref[0] = part(1)
    last_ref[0] = part(3)

    @pl.when(step < middle)
    def _():
        low_ref[0] = part(2)

    @pl.when(step >= middle)
    def _():
        high_ref[0] = part(2)


def proj_terms(ids, pieces, ot):
    count, width, _ = ot.shape
    far, near = GRID["dp"], GRID["fsdp"]
    depth = pieces[0].shape[1]
    middle = far // 2
    block = (1, width, TOK)

    def plane(i, ids):
        return (i, 0, 0)

    full = jax.ShapeDtypeStruct((far, width, TOK), BF16)
    part = jax.ShapeDtypeStruct((middle, width, TOK), BF16)
    return pl.pallas_call(
        proj_kernel,
        grid_spec=pltpu.PrefetchScalarGridSpec(
            num_scalar_prefetch=1,
            grid=(far,),
            in_specs=[pl.BlockSpec((TOK, near * TOK), lambda i, ids: (0, i))] * count
            + [pl.BlockSpec(ot.shape, lambda i, ids: (0, 0, 0))],
            out_specs=[
                pl.BlockSpec(block, plane),
                pl.BlockSpec(block, plane),
                pl.BlockSpec(block, lambda i, ids: (jnp.minimum(i, middle - 1), 0, 0)),
                pl.BlockSpec(block, lambda i, ids: (jnp.maximum(i - middle, 0), 0, 0)),
                pl.BlockSpec(block, plane),
            ],
            scratch_shapes=[
                pltpu.VMEM((width, count * TOK), BF16),
                pltpu.VMEM((width, near * TOK), BF16),
            ],
        ),
        out_shape=[full, full, part, part, full],
        cost_estimate=pl.CostEstimate(
            flops=2 * count * TOK * width * depth,
            bytes_accessed=2 * (count * TOK * (depth + width) + depth * width),
            transcendentals=0,
        ),
        name="proj_terms",
    )(ids, *pieces, ot)


def join_kernel(low_ref, up_ref, high_ref, down_ref, low_out, high_out):
    low_out[...] = add(low_ref[...], up_ref[...])
    high_out[...] = add(high_ref[...], down_ref[...])


def join(low, up, high, down):
    planes, width, _ = up.shape
    block = (planes // 2, width, TOK)

    def front(i):
        return (i, 0, 0)

    def back(i):
        return (i + 2, 0, 0)

    return pl.pallas_call(
        join_kernel,
        grid=(2,),
        in_specs=[
            pl.BlockSpec(block, front),
            pl.BlockSpec(block, front),
            pl.BlockSpec(block, back),
            pl.BlockSpec(block, front),
        ],
        out_specs=[pl.BlockSpec(block, front), pl.BlockSpec(block, back)],
        out_shape=[jax.ShapeDtypeStruct(low.shape, BF16)] * 2,
        input_output_aliases={0: 0, 2: 1},
        cost_estimate=pl.CostEstimate(
            flops=2 * up.size, bytes_accessed=12 * up.size, transcendentals=0
        ),
        name="join",
    )(low, up, high, down)


def shift(x, axis, by):
    n = GRID[axis]
    return lax.ppermute(x, axis, [(i, (i + by) % n) for i in range(n)])


def add(a, b):
    return (a.astype(F32) + b.astype(F32)).astype(BF16)


def after(value, done):
    return lax.optimization_barrier((value, done))[0]


def swap(x, axis):
    return lax.all_to_all(x, axis, split_axis=0, concat_axis=0, tiled=True)


def hop(x, chips, core):
    pairs = [(i * 2 + c, ((i + chips) % 4) * 2 + (c ^ core)) for i in range(4) for c in range(2)]
    return lax.ppermute(x, "seq", pairs)


def per_device(
    query_rows, forward_key_rows, forward_value_rows, out_cotangent, proj_weight, sent_lengths
):
    place = lax.axis_index("seq").astype(jnp.int32)
    chip, core = place // 2, place % 2
    chips = (chip + jnp.array([0, 3, 1, 2], jnp.int32)) % 4 * 2
    ids = jnp.concatenate(
        [
            chips + core,
            chips + 1 - core,
            jnp.stack([lax.axis_index("dp"), lax.axis_index("fsdp")]).astype(jnp.int32),
        ]
    )
    targets = (chip + jnp.array([0, 1, 3, 2], jnp.int32)) % 4 * 2
    targets = jnp.concatenate([targets + core, targets + 1 - core])
    far = GRID["dp"] // 2
    half = TOK // 2
    own = out_cotangent[0]
    left, right = hop(own, 1, 0), hop(own, -1, 0)
    weight = jnp.broadcast_to(proj_weight, (2 * far, *proj_weight.shape))
    weight = swap(weight, "dp")
    packed = pack(targets, query_rows, forward_key_rows, forward_value_rows)
    paths = [(chips, flip) for flip in range(2) for chips in (0, 1, -1, 2)]
    packed = [packed[0]] + [hop(x, *path) for x, path in zip(packed[1:], paths[1:])]
    partner = hop(own, 0, 1)
    below, above = shift(weight, "fsdp", 1), shift(weight, "fsdp", -1)
    lo, hi = limits(sent_lengths[0], len(packed))
    across = [hop(left[:half], 1, 0), hop(right[half:], -1, 0)]
    across = jnp.concatenate(across, 0)
    output = attend(ids, packed, lo, hi)
    pieces = [own, left, right, across, partner]
    pieces += [hop(piece, 0, 1) for piece in (left, right, across)]
    same, following, low, high, before = proj_terms(ids, pieces, output)
    up, down = shift(low, "fsdp", 1), shift(high, "fsdp", -1)
    below, above = after((below, above), low)
    ends = [shift(below[:far], "fsdp", 1), shift(above[far:], "fsdp", -1)]
    sums, rows = upstream_most(ids, pieces, [weight, below, above])
    following, before = join(following, up, before, down)
    up, down = shift(following, "fsdp", 1), shift(before, "fsdp", -1)
    arriving = upstream_rest(ids, rows, ends, sums)
    grads = attend_grad(jnp.concatenate([ids, targets]), packed, arriving, lo, hi)
    up, down = after((up, down), grads[0])
    first = (same.astype(F32) + up.astype(F32) + down.astype(F32)).astype(BF16)
    first = swap(first, "dp")
    grads = [grads[0]] + [hop(x, *path) for x, path in zip(grads[1:], paths[1:])]
    proj_grad = jnp.sum(first.astype(F32), axis=0).T.astype(BF16)
    query_grad, key_gradient, value_gradient = unpack(ids, grads)
    return (query_grad, key_gradient, value_gradient, proj_grad)


def solution(mesh):
    in_specs = (
        P(("dp", "fsdp"), "seq", None),
        P(("dp", "fsdp"), "seq", None),
        P(("dp", "fsdp"), "seq", None),
        P(("dp", "fsdp"), "seq", None),
        P(("dp", "fsdp"), "seq"),
        P(("dp", "fsdp"), None),
    )
    out_specs = (
        P(("dp", "fsdp"), "seq", None),
        P(("dp", "fsdp"), "seq", None),
        P(("dp", "fsdp"), "seq", None),
        P(("dp", "fsdp"), "seq"),
    )
    return jax.shard_map(
        per_device, mesh=mesh, in_specs=in_specs, out_specs=out_specs, check_vma=False
    )
```

```python
import math

import jax
import jax.numpy as jnp
from jax import lax
from jax.experimental import pallas as pl
from jax.experimental.pallas import tpu as pltpu
from jax.sharding import PartitionSpec as P

HEADS = 4
HEAD = 128
TOK = 128
KW = 448
FACTOR = 1.0 / math.sqrt(HEAD)
F32 = jnp.float32
BF16 = jnp.bfloat16
GROUP = 4
GRID = {"dp": 8, "fsdp": 4}


def window_start(i, blocks):
    return pl.multiple_of(jnp.clip(i * TOK - 256, 0, blocks * TOK - KW), 64)


def probs(i, start, q_ref, lo_ref, hi_ref, key, h0):
    q = jnp.concatenate(
        [q_ref[i, :, (h0 + j) * HEAD : (h0 + j + 1) * HEAD] for j in range(GROUP)], 0
    )
    s = lax.dot_general(key, q, (((1,), (1,)), ((), ())), preferred_element_type=F32)
    place = start + lax.broadcasted_iota(jnp.int32, (KW, GROUP * TOK), 0)
    lo = jnp.concatenate([lo_ref[i]] * GROUP, 1)
    hi = jnp.concatenate([hi_ref[i]] * GROUP, 1)
    p = jnp.where((place >= lo) & (place < hi), jnp.exp(s * FACTOR), 0.0)
    a = p * (1.0 / jnp.sum(p, axis=0, keepdims=True))
    return q, a


def assemble(ids_ref, pieces, q_ref, k_ref, v_ref):
    for p, piece in enumerate(pieces):
        b = ids_ref[p]
        rows = pl.ds(pl.multiple_of(b * TOK, TOK), TOK)
        q_ref[b] = piece[:, : HEADS * HEAD]
        k_ref[rows, :] = piece[:, HEADS * HEAD : (HEADS + 1) * HEAD]
        v_ref[rows, :] = piece[:, (HEADS + 1) * HEAD :]


def fwd_kernel(ids_ref, *refs):
    pieces, (lo_ref, hi_ref, o_ref, q_ref, k_ref, v_ref) = refs[:-6], refs[-6:]
    blocks = len(pieces)
    i = pl.program_id(0)

    @pl.when(i == 0)
    def _():
        assemble(ids_ref, pieces, q_ref, k_ref, v_ref)

    start = window_start(i, blocks)
    key = k_ref[pl.ds(start, KW), :]
    vt = v_ref[pl.ds(start, KW), :].T
    for h0 in range(0, HEADS, GROUP):
        _, a = probs(i, start, q_ref, lo_ref, hi_ref, key, h0)
        o = jnp.dot(vt, a.astype(BF16), preferred_element_type=F32).astype(BF16)
        for j in range(GROUP):
            o_ref[0, (h0 + j) * HEAD : (h0 + j + 1) * HEAD, :] = o[:, j * TOK : (j + 1) * TOK]


def bwd_kernel(ids_ref, *refs):
    blocks = (len(refs) - 9) // 2
    pieces, (u_ref, lo_ref, hi_ref) = refs[:blocks], refs[blocks : blocks + 3]
    homes, scratch = refs[blocks + 3 : -6], refs[-6:]
    o_ref, dk_ref, dv_ref, q_ref, k_ref, v_ref = scratch
    i = pl.program_id(0)

    @pl.when(i == 0)
    def _():
        assemble(ids_ref, pieces, q_ref, k_ref, v_ref)
        dk_ref[...] = jnp.zeros_like(dk_ref)
        dv_ref[...] = jnp.zeros_like(dv_ref)

    start = window_start(i, blocks)
    key = k_ref[pl.ds(start, KW), :]
    val = v_ref[pl.ds(start, KW), :]
    kt = key.T
    dk = None
    for h0 in range(0, HEADS, GROUP):
        q, a = probs(i, start, q_ref, lo_ref, hi_ref, key, h0)
        u = jnp.concatenate(
            [u_ref[i, :, (h0 + j) * HEAD : (h0 + j + 1) * HEAD] for j in range(GROUP)], 0
        )
        g = lax.dot_general(val, u, (((1,), (1,)), ((), ())), preferred_element_type=F32)
        delta = jnp.sum(a * g, axis=0, keepdims=True)
        ds = (a * (g - delta) * FACTOR).astype(BF16)
        dq = jnp.dot(kt, ds, preferred_element_type=F32)
        for j in range(GROUP):
            o_ref[i, :, (h0 + j) * HEAD : (h0 + j + 1) * HEAD] = dq[
                :, j * TOK : (j + 1) * TOK
            ].T.astype(BF16)
        dkh = jnp.dot(ds, q, preferred_element_type=F32)
        dvh = jnp.dot(a.astype(BF16), u, preferred_element_type=F32)
        dk, dv = (dkh, dvh) if dk is None else (dk + dkh, dv + dvh)
    dk_ref[pl.ds(start, KW), :] += dk
    dv_ref[pl.ds(start, KW), :] += dv

    @pl.when(i == blocks - 1)
    def _():
        for p, home in enumerate(homes):
            b = ids_ref[blocks + 2 + p]
            rows = pl.ds(pl.multiple_of(b * TOK, TOK), TOK)
            home[:, : HEADS * HEAD] = o_ref[b]
            home[:, HEADS * HEAD : (HEADS + 1) * HEAD] = dk_ref[rows, :].astype(BF16)
            home[:, (HEADS + 1) * HEAD :] = dv_ref[rows, :].astype(BF16)


def whole(shape):
    return pl.BlockSpec(shape, lambda i, ids: (0,) * len(shape))


def limits(sent_lengths, blocks):
    number = sent_lengths.shape[0]
    order = jnp.arange(number, dtype=jnp.int32)
    ends = jnp.sum(jnp.where(order[None, :] <= order[:, None], sent_lengths[None, :], 0), axis=1)
    places = jnp.arange(blocks * TOK, dtype=jnp.int32)
    sentence = jnp.sum((places[:, None] >= ends[None, :]).astype(jnp.int32), axis=1)
    lo = jnp.sum(
        jnp.where(order[None, :] + 3 < sentence[:, None], sent_lengths[None, :], 0), axis=1
    )
    hi = jnp.sum(jnp.where(order[None, :] <= sentence[:, None], sent_lengths[None, :], 0), axis=1)
    return lo.reshape(blocks, 1, TOK), hi.reshape(blocks, 1, TOK)


def head_scratch(blocks):
    keys = pltpu.VMEM((blocks * TOK, HEAD), BF16)
    return [pltpu.VMEM((blocks, TOK, HEADS * HEAD), BF16), keys, keys]


def attend(ids, pieces, lo, hi):
    blocks = len(pieces)
    pairs = blocks * TOK * KW * HEADS
    return pl.pallas_call(
        fwd_kernel,
        grid_spec=pltpu.PrefetchScalarGridSpec(
            num_scalar_prefetch=1,
            grid=(blocks,),
            in_specs=[whole(x.shape) for x in (*pieces, lo, hi)],
            out_specs=pl.BlockSpec((1, HEADS * HEAD, TOK), lambda i, ids: (i, 0, 0)),
            scratch_shapes=head_scratch(blocks),
        ),
        out_shape=jax.ShapeDtypeStruct((blocks, HEADS * HEAD, TOK), BF16),
        cost_estimate=pl.CostEstimate(
            flops=4 * pairs * HEAD,
            bytes_accessed=4 * blocks * pieces[0].size,
            transcendentals=pairs,
        ),
        name="attend",
    )(ids, *pieces, lo, hi)


def attend_grad(ids, pieces, u, lo, hi):
    blocks = len(pieces)
    pairs = blocks * TOK * KW * HEADS
    shape = pieces[0].shape
    return pl.pallas_call(
        bwd_kernel,
        grid_spec=pltpu.PrefetchScalarGridSpec(
            num_scalar_prefetch=1,
            grid=(blocks,),
            in_specs=[whole(x.shape) for x in (*pieces, u, lo, hi)],
            out_specs=[whole(shape)] * blocks,
            scratch_shapes=[pltpu.VMEM((blocks, TOK, HEADS * HEAD), BF16)]
            + [pltpu.VMEM((blocks * TOK, HEAD), F32)] * 2
            + head_scratch(blocks),
        ),
        out_shape=[jax.ShapeDtypeStruct(shape, BF16)] * blocks,
        cost_estimate=pl.CostEstimate(
            flops=10 * pairs * HEAD,
            bytes_accessed=6 * blocks * pieces[0].size,
            transcendentals=pairs,
        ),
        name="attend_grad",
    )(ids, *pieces, u, lo, hi)


def pack_kernel(ids_ref, q_ref, k_ref, v_ref, *o_refs):
    wide = HEADS * HEAD
    for p, o_ref in enumerate(o_refs):
        g = ids_ref[p]
        heads = pl.ds(pl.multiple_of(g * HEAD, HEAD), HEAD)
        o_ref[:, :wide] = q_ref[0, :, pl.ds(pl.multiple_of(g * wide, wide), wide)]
        o_ref[:, wide : wide + HEAD] = k_ref[0, :, heads]
        o_ref[:, wide + HEAD :] = v_ref[0, :, heads]


def pack(ids, q, k, v):
    groups = k.shape[2] // HEAD
    width = (HEADS + 2) * HEAD
    return pl.pallas_call(
        pack_kernel,
        grid_spec=pltpu.PrefetchScalarGridSpec(
            num_scalar_prefetch=1,
            grid=(1,),
            in_specs=[whole(x.shape) for x in (q, k, v)],
            out_specs=[whole((TOK, width))] * groups,
        ),
        out_shape=[jax.ShapeDtypeStruct((TOK, width), BF16)] * groups,
        cost_estimate=pl.CostEstimate(flops=0, bytes_accessed=6 * q.size, transcendentals=0),
        name="pack",
    )(ids, q, k, v)


def unpack_kernel(ids_ref, *refs):
    wide = HEADS * HEAD
    pieces, (q_ref, k_ref, v_ref) = refs[:-3], refs[-3:]
    for p, piece in enumerate(pieces):
        g = ids_ref[p]
        heads = pl.ds(pl.multiple_of(g * HEAD, HEAD), HEAD)
        q_ref[0, :, pl.ds(pl.multiple_of(g * wide, wide), wide)] = piece[:, :wide]
        k_ref[0, :, heads] = piece[:, wide : wide + HEAD]
        v_ref[0, :, heads] = piece[:, wide + HEAD :]


def unpack(ids, pieces):
    groups = len(pieces)
    shapes = [(1, TOK, groups * part) for part in (HEADS * HEAD, HEAD, HEAD)]
    return pl.pallas_call(
        unpack_kernel,
        grid_spec=pltpu.PrefetchScalarGridSpec(
            num_scalar_prefetch=1,
            grid=(1,),
            in_specs=[whole(x.shape) for x in pieces],
            out_specs=[whole(shape) for shape in shapes],
        ),
        out_shape=[jax.ShapeDtypeStruct(shape, BF16) for shape in shapes],
        cost_estimate=pl.CostEstimate(
            flops=0, bytes_accessed=4 * groups * pieces[0].size, transcendentals=0
        ),
        name="unpack",
    )(ids, *pieces)


def gathered_rows(ids_ref, pieces, offsets):
    near = GRID["fsdp"]
    planes = pieces[0].shape[1] // (near * TOK)
    turn = ids_ref[len(pieces) + 1]
    starts = [
        pl.multiple_of((plane * near + lax.rem(turn + offset, near)) * TOK, TOK)
        for offset in offsets
        for plane in range(planes)
    ]
    return jnp.concatenate(
        [
            jnp.concatenate([piece[:, pl.ds(start, TOK)] for start in starts], 1)
            for piece in pieces
        ],
        0,
    )


def most_kernel(ids_ref, *refs):
    pieces, (mine_ref, below_ref, above_ref, o_ref, left_ref) = refs[:-5], refs[-5:]
    near = GRID["fsdp"]
    left_ref[...] = gathered_rows(ids_ref, pieces, (2,))
    rows = gathered_rows(ids_ref, pieces, (0, near - 1, 1))
    width = mine_ref.shape[2]
    weight = jnp.concatenate(
        [x[...].reshape(-1, width) for x in (mine_ref, below_ref, above_ref)], 0
    )
    part = jnp.dot(rows, weight, preferred_element_type=F32)
    first = pl.program_id(0) == 0

    @pl.when(first)
    def _():
        o_ref[...] = part

    @pl.when(jnp.logical_not(first))
    def _():
        o_ref[...] += part


def rest_kernel(ids_ref, rows_ref, low_ref, high_ref, sum_ref, o_ref):
    width = low_ref.shape[2]
    weight = jnp.concatenate([x[...].reshape(-1, width) for x in (low_ref, high_ref)], 0)
    total = sum_ref[...] + jnp.dot(rows_ref[...], weight, preferred_element_type=F32)
    count = rows_ref.shape[0] // TOK
    first = pl.program_id(0) * count
    for p in range(count):
        o_ref[ids_ref[first + p]] = total[p * TOK : (p + 1) * TOK, :].astype(BF16)


PLANES = 2


def chunk_specs(pieces):
    near = GRID["fsdp"]
    return [pl.BlockSpec((TOK, PLANES * near * TOK), lambda i, ids: (0, i))] * len(pieces)


def upstream_most(ids, pieces, weights):
    far, rows, width = weights[0].shape
    count = len(pieces)
    tokens = count * TOK
    depth = 3 * far * rows
    return pl.pallas_call(
        most_kernel,
        grid_spec=pltpu.PrefetchScalarGridSpec(
            num_scalar_prefetch=1,
            grid=(far // PLANES,),
            in_specs=chunk_specs(pieces)
            + [pl.BlockSpec((PLANES, rows, width), lambda i, ids: (i, 0, 0))] * 3,
            out_specs=[
                whole((tokens, width)),
                pl.BlockSpec((tokens, PLANES * TOK), lambda i, ids: (0, i)),
            ],
        ),
        out_shape=[
            jax.ShapeDtypeStruct((tokens, width), F32),
            jax.ShapeDtypeStruct((tokens, far * TOK), BF16),
        ],
        cost_estimate=pl.CostEstimate(
            flops=2 * tokens * width * depth,
            bytes_accessed=2 * (tokens * (depth + 2 * width) + depth * width),
            transcendentals=0,
        ),
        name="upstream_most",
    )(ids, *pieces, *weights)


def upstream_rest(ids, rows, ends, sums):
    tokens, depth = rows.shape
    width = sums.shape[1]
    steps = 2
    return pl.pallas_call(
        rest_kernel,
        grid_spec=pltpu.PrefetchScalarGridSpec(
            num_scalar_prefetch=1,
            grid=(steps,),
            in_specs=[
                pl.BlockSpec((tokens // steps, depth), lambda i, ids: (i, 0)),
                whole(ends[0].shape),
                whole(ends[1].shape),
                pl.BlockSpec((tokens // steps, width), lambda i, ids: (i, 0)),
            ],
            out_specs=whole((tokens // TOK, TOK, width)),
        ),
        out_shape=jax.ShapeDtypeStruct((tokens // TOK, TOK, width), BF16),
        cost_estimate=pl.CostEstimate(
            flops=2 * tokens * width * depth,
            bytes_accessed=2 * (tokens * (depth + 3 * width) + depth * width),
            transcendentals=0,
        ),
        name="upstream_rest",
    )(ids, rows, *ends, sums)


def proj_kernel(ids_ref, *refs):
    pieces, refs = refs[:-8], refs[-8:]
    ot_ref, same_ref, next_ref, low_ref, high_ref, last_ref, lhs_ref, out_ref = refs
    count = len(pieces)
    near = GRID["fsdp"]
    step = pl.program_id(0)
    middle = pl.num_programs(0) // 2

    @pl.when(step == 0)
    def _():
        for p in range(count):
            lhs_ref[:, p * TOK : (p + 1) * TOK] = ot_ref[ids_ref[p]]

    rows = jnp.concatenate([piece[...] for piece in pieces], 0)
    out_ref[...] = jnp.dot(lhs_ref[...], rows, preferred_element_type=F32).astype(BF16)

    def fill(ref, offset):
        t = lax.rem(ids_ref[count + 1] + offset, near)
        for plane in range(PLANES):
            start = pl.multiple_of((plane * near + t) * TOK, TOK)
            ref[plane] = out_ref[:, pl.ds(start, TOK)]

    fill(same_ref, 0)
    fill(next_ref, 1)
    fill(last_ref, 3)

    @pl.when(step < middle)
    def _():
        fill(low_ref, 2)

    @pl.when(step >= middle)
    def _():
        fill(high_ref, 2)


def proj_terms(ids, pieces, ot):
    count, width, _ = ot.shape
    far, near = GRID["dp"], GRID["fsdp"]
    depth = pieces[0].shape[1]
    steps = far // PLANES
    middle = steps // 2
    block = (PLANES, width, TOK)

    def plane(i, ids):
        return (i, 0, 0)

    full = jax.ShapeDtypeStruct((far, width, TOK), BF16)
    part = jax.ShapeDtypeStruct((far // 2, width, TOK), BF16)
    return pl.pallas_call(
        proj_kernel,
        grid_spec=pltpu.PrefetchScalarGridSpec(
            num_scalar_prefetch=1,
            grid=(steps,),
            in_specs=chunk_specs(pieces)
            + [pl.BlockSpec(ot.shape, lambda i, ids: (0, 0, 0))],
            out_specs=[
                pl.BlockSpec(block, plane),
                pl.BlockSpec(block, plane),
                pl.BlockSpec(block, lambda i, ids: (jnp.minimum(i, middle - 1), 0, 0)),
                pl.BlockSpec(block, lambda i, ids: (jnp.maximum(i - middle, 0), 0, 0)),
                pl.BlockSpec(block, plane),
            ],
            scratch_shapes=[
                pltpu.VMEM((width, count * TOK), BF16),
                pltpu.VMEM((width, PLANES * near * TOK), BF16),
            ],
        ),
        out_shape=[full, full, part, part, full],
        cost_estimate=pl.CostEstimate(
            flops=2 * count * TOK * width * depth,
            bytes_accessed=2 * (count * TOK * (depth + width) + depth * width),
            transcendentals=0,
        ),
        name="proj_terms",
    )(ids, *pieces, ot)


def join_kernel(low_ref, up_ref, high_ref, down_ref, low_out, high_out):
    low_out[...] = add(low_ref[...], up_ref[...])
    high_out[...] = add(high_ref[...], down_ref[...])


def join(low, up, high, down):
    planes, width, _ = up.shape
    block = (planes // 2, width, TOK)

    def front(i):
        return (i, 0, 0)

    def back(i):
        return (i + 2, 0, 0)

    return pl.pallas_call(
        join_kernel,
        grid=(2,),
        in_specs=[
            pl.BlockSpec(block, front),
            pl.BlockSpec(block, front),
            pl.BlockSpec(block, back),
            pl.BlockSpec(block, front),
        ],
        out_specs=[pl.BlockSpec(block, front), pl.BlockSpec(block, back)],
        out_shape=[jax.ShapeDtypeStruct(low.shape, BF16)] * 2,
        input_output_aliases={0: 0, 2: 1},
        cost_estimate=pl.CostEstimate(
            flops=2 * up.size, bytes_accessed=12 * up.size, transcendentals=0
        ),
        name="join",
    )(low, up, high, down)


def shift(x, axis, by):
    n = GRID[axis]
    return lax.ppermute(x, axis, [(i, (i + by) % n) for i in range(n)])


def add(a, b):
    return (a.astype(F32) + b.astype(F32)).astype(BF16)


def after(value, done):
    return lax.optimization_barrier((value, done))[0]


def swap(x, axis):
    return lax.all_to_all(x, axis, split_axis=0, concat_axis=0, tiled=True)


def hop(x, chips, core):
    pairs = [(i * 2 + c, ((i + chips) % 4) * 2 + (c ^ core)) for i in range(4) for c in range(2)]
    return lax.ppermute(x, "seq", pairs)


def per_device(
    query_rows, forward_key_rows, forward_value_rows, out_cotangent, proj_weight, sent_lengths
):
    place = lax.axis_index("seq").astype(jnp.int32)
    chip, core = place // 2, place % 2
    chips = (chip + jnp.array([0, 3, 1, 2], jnp.int32)) % 4 * 2
    ids = jnp.concatenate(
        [
            chips + core,
            chips + 1 - core,
            jnp.stack([lax.axis_index("dp"), lax.axis_index("fsdp")]).astype(jnp.int32),
        ]
    )
    targets = (chip + jnp.array([0, 1, 3, 2], jnp.int32)) % 4 * 2
    targets = jnp.concatenate([targets + core, targets + 1 - core])
    far = GRID["dp"] // 2
    half = TOK // 2
    own = out_cotangent[0]
    left, right = hop(own, 1, 0), hop(own, -1, 0)
    weight = jnp.broadcast_to(proj_weight, (2 * far, *proj_weight.shape))
    weight = swap(weight, "dp")
    packed = pack(targets, query_rows, forward_key_rows, forward_value_rows)
    paths = [(chips, flip) for flip in range(2) for chips in (0, 1, -1, 2)]
    packed = [packed[0]] + [hop(x, *path) for x, path in zip(packed[1:], paths[1:])]
    partner = hop(own, 0, 1)
    below, above = shift(weight, "fsdp", 1), shift(weight, "fsdp", -1)
    lo, hi = limits(sent_lengths[0], len(packed))
    across = [hop(left[:half], 1, 0), hop(right[half:], -1, 0)]
    across = jnp.concatenate(across, 0)
    output = attend(ids, packed, lo, hi)
    pieces = [own, left, right, across, partner]
    pieces += [hop(piece, 0, 1) for piece in (left, right, across)]
    same, following, low, high, before = proj_terms(ids, pieces, output)
    up, down = shift(low, "fsdp", 1), shift(high, "fsdp", -1)
    below, above = after((below, above), low)
    ends = [shift(below[:far], "fsdp", 1), shift(above[far:], "fsdp", -1)]
    sums, rows = upstream_most(ids, pieces, [weight, below, above])
    following, before = join(following, up, before, down)
    up, down = shift(following, "fsdp", 1), shift(before, "fsdp", -1)
    arriving = upstream_rest(ids, rows, ends, sums)
    grads = attend_grad(jnp.concatenate([ids, targets]), packed, arriving, lo, hi)
    up, down = after((up, down), grads[0])
    first = (same.astype(F32) + up.astype(F32) + down.astype(F32)).astype(BF16)
    first = swap(first, "dp")
    grads = [grads[0]] + [hop(x, *path) for x, path in zip(grads[1:], paths[1:])]
    proj_grad = jnp.sum(first.astype(F32), axis=0).T.astype(BF16)
    query_grad, key_gradient, value_gradient = unpack(ids, grads)
    return (query_grad, key_gradient, value_gradient, proj_grad)


def solution(mesh):
    in_specs = (
        P(("dp", "fsdp"), "seq", None),
        P(("dp", "fsdp"), "seq", None),
        P(("dp", "fsdp"), "seq", None),
        P(("dp", "fsdp"), "seq", None),
        P(("dp", "fsdp"), "seq"),
        P(("dp", "fsdp"), None),
    )
    out_specs = (
        P(("dp", "fsdp"), "seq", None),
        P(("dp", "fsdp"), "seq", None),
        P(("dp", "fsdp"), "seq", None),
        P(("dp", "fsdp"), "seq"),
    )
    return jax.shard_map(
        per_device, mesh=mesh, in_specs=in_specs, out_specs=out_specs, check_vma=False
    )
```
